128 devices in a mesh: seq: 16 (over x, z), guid: 2 (over core), tp: 4 (over y).
Axes of the slice: x: 4, y: 4, z: 4, core: 2. Of those that a mesh axis runs over, the one named last changes fastest.
Arguments:
- hidden_states: bfloat16 [2, 6144, 3072], P('guid', 'seq'), may hold values from -6 to 6
- modulation: float32 [2, 3, 3072], P('guid')
- w_query: bfloat16 [3072, 3072], P(None, 'tp'), may hold values from -0.109375 to 0.109375
- w_key: bfloat16 [3072, 3072], P(None, 'tp'), may hold values from -0.109375 to 0.109375
- w_value: bfloat16 [3072, 3072], P(None, 'tp'), may hold values from -0.109375 to 0.109375
- w_out: bfloat16 [3072, 3072], P('tp'), may hold values from -0.109375 to 0.109375
- block_ids: int32 [48, 12], P('seq'), may hold values from 0 to 47, as said below
- block_count: int32 [48], P('seq'), may hold values from 1 to 12, as said below
- guidance: float32 [1], replicated, may hold values from 4 to 8
Outputs:
- guided: bfloat16 [6144, 3072], P('seq', ('guid', 'tp'))
The draws below stay inside these ranges and needn't reach their ends.
Inputs may be any that keep to these rules, and one draw needn't show every extreme that they name: `block_ids`: entry 0 of each list is the query tile itself; the first block_count entries are distinct tiles within 12 tiles of the query tile; later entries repeat the query tile. `block_count`: some query tile lists 12 tiles.
All inputs are finite; a program needn't handle non-finite values.
Results may differ from the reference program's by a relative error of at most 0.02.
The reference program's roundings to bfloat16 on the way count: a program that leaves them out, or rounds other values in their place, can miss the bound.
Values may be sent and summed in bfloat16 or wider, within the bound.
A program may use at most 192 MiB of HBM per device.

```python
import jax
import jax.numpy as jnp
from jax import lax

D = 3072
HEADS = 48
HD = 64
TILE = 128
TOKENS = 6144
TILES = 48
REACH = 12
KMAX = 12


def mask_tables(key):
    base = jax.random.fold_in(key, 7)
    first_key, second_key = jax.random.split(base, 2)
    span = 2 * REACH + 1
    offsets = jnp.arange(span, dtype=jnp.int32) - REACH
    row_keys = jax.random.split(first_key, TILES)
    ranks = jax.vmap(lambda one: jax.random.permutation(one, span))(row_keys).astype(jnp.int32)
    rows = jnp.arange(TILES, dtype=jnp.int32)
    index = rows[:, None] + offsets[None, :]
    valid = (index >= 0) & (index < TILES)
    order_key = jnp.where(offsets[None, :] == 0, -1, jnp.where(valid, ranks, ranks + span))
    order = jnp.argsort(order_key, axis=1, stable=True)
    picked = jnp.take_along_axis(index, order, axis=1)[:, :KMAX]
    counted = jax.random.randint(second_key, (TILES,), 1, KMAX + 1).astype(jnp.int32)
    counted = jnp.minimum(counted, jnp.sum(valid.astype(jnp.int32), axis=1))
    counted = jnp.where(rows == TILES // 2, KMAX, counted).astype(jnp.int32)
    slots = jnp.arange(KMAX, dtype=jnp.int32)[None, :]
    listed = jnp.where(slots < counted[:, None], picked, rows[:, None]).astype(jnp.int32)
    return (listed, counted)


def draw_block_ids(key, part):
    return mask_tables(key)[0]


def draw_block_count(key, part):
    return mask_tables(key)[1]


def draw_modulation(key, part):
    base = jax.random.fold_in(key, 11)
    k_shift, k_scale, k_gate = jax.random.split(base, 3)
    shift = 0.5 * jax.random.normal(k_shift, (2, D), jnp.float32)
    gate = 1.0 + 0.5 * jax.random.normal(k_gate, (2, D), jnp.float32)
    scale = 0.5 * jax.random.normal(k_scale, (2, D), jnp.float32)
    return jnp.stack([shift, scale, gate], axis=1).astype(jnp.float32)


def level_of(own_key, dims, pieces, least, top_value):
    def one(position, parts):
        heights = jax.random.uniform(jax.random.fold_in(jax.random.fold_in(own_key, 6), position), (parts,), jnp.float32, least / len(pieces), top_value / len(pieces))
        return jnp.repeat(jnp.exp(heights), dims[position] // parts).reshape((-1,) + (1,) * (len(dims) - position - 1))

    level = one(*pieces[0])
    for cut in pieces[1:]:
        level = level * one(*cut)
    return level


def gaussian(rng, extent, scale, limit, shards=(), kind=jnp.bfloat16):
    values = scale * jax.random.normal(rng, extent, jnp.float32)
    if shards:
        values = values * level_of(rng, extent, shards, -0.22, 0.18)
    return jnp.clip(values, -limit, limit).astype(kind)


def setup_inputs(seed: int = 0) -> dict:
    arg_keys = jax.random.split(jax.random.key(seed), 10)
    return {
        "hidden_states": gaussian(arg_keys[0], (2, TOKENS, D), 1.0, 6.0, ((0, 2), (1, 16))),
        "modulation": draw_modulation(jax.random.fold_in(arg_keys[9], 71), 0),
        "w_query": gaussian(arg_keys[2], (D, HEADS * HD), D ** -0.5, 0.109375, ((1, 4),)),
        "w_key": gaussian(arg_keys[3], (D, HEADS * HD), D ** -0.5, 0.109375, ((1, 4),)),
        "w_value": gaussian(arg_keys[4], (D, HEADS * HD), D ** -0.5, 0.109375, ((1, 4),)),
        "w_out": gaussian(arg_keys[5], (HEADS * HD, D), (HEADS * HD) ** -0.5, 0.109375, ((0, 4),)),
        "block_ids": draw_block_ids(jax.random.fold_in(arg_keys[9], 71), 0),
        "block_count": draw_block_count(jax.random.fold_in(arg_keys[9], 71), 0),
        "guidance": jnp.clip(jax.random.uniform(arg_keys[8], (1,), jnp.float32, 4.0, 8.0), 4.0, 8.0),
    }


def tile_table(block_ids, block_count):
    live = jnp.arange(block_ids.shape[1], dtype=jnp.int32)[None, :] < block_count[:, None]
    every = jnp.arange(TILES, dtype=jnp.int32)
    hit = (block_ids[:, :, None] == every[None, None, :]) & live[:, :, None]
    return jnp.any(hit, axis=1).astype(jnp.int32)

def one_branch(states, modul, w_query, w_key, w_value, w_out, allowed):
    xf = states.astype(jnp.float32)
    mean = lax.optimization_barrier(jnp.mean(xf, axis=1, keepdims=True))
    var = lax.optimization_barrier(jnp.mean((xf - mean) ** 2, axis=1, keepdims=True))
    normed = (xf - mean) / jnp.sqrt(var + 1e-05)
    h = (normed * (1.0 + modul[1]) + modul[0]).astype(jnp.bfloat16)
    query = lax.optimization_barrier(jnp.dot(h, w_query, preferred_element_type=jnp.float32).astype(jnp.bfloat16)).astype(jnp.float32)
    keys = lax.optimization_barrier(jnp.dot(h, w_key, preferred_element_type=jnp.float32).astype(jnp.bfloat16)).astype(jnp.float32)
    values = lax.optimization_barrier(jnp.dot(h, w_value, preferred_element_type=jnp.float32).astype(jnp.bfloat16)).astype(jnp.float32)
    span = min(2 * REACH + 1, TILES)

    def one_tile(tile_idx):
        rows = lax.dynamic_slice_in_dim(query, tile_idx * TILE, TILE, 0).reshape(TILE, HEADS, HD)
        first = jnp.clip(tile_idx - REACH, 0, TILES - span).astype(jnp.int32)
        near_k = lax.dynamic_slice_in_dim(keys, first * TILE, span * TILE, 0).reshape(span * TILE, HEADS, HD)
        near_v = lax.dynamic_slice_in_dim(values, first * TILE, span * TILE, 0).reshape(span * TILE, HEADS, HD)
        tile_ok = lax.dynamic_slice_in_dim(allowed[tile_idx], first, span, 0) > 0
        mask = jnp.repeat(tile_ok, TILE)[None, None, :]
        scores = jnp.einsum('qhd,khd->hqk', rows, near_k) * 0.125
        scores = jnp.where(mask, scores, -1e+30)
        top = lax.optimization_barrier(jnp.max(scores, axis=2, keepdims=True))
        expo = jnp.where(mask, jnp.exp(scores - top), 0.0)
        total = lax.optimization_barrier(jnp.sum(expo, axis=2))
        rounded = lax.optimization_barrier(expo.astype(jnp.bfloat16)).astype(jnp.float32)
        summed = jnp.einsum('hqk,khd->qhd', rounded, near_v)
        result = summed / jnp.transpose(total)[:, :, None]
        return result.reshape(TILE, HEADS * HD).astype(jnp.bfloat16)
    attn = lax.map(one_tile, jnp.arange(TILES, dtype=jnp.int32)).reshape(TOKENS, HEADS * HD)
    proj = jnp.dot(attn, w_out, preferred_element_type=jnp.float32)
    return xf + modul[2] * proj

def reference(hidden_states, modulation, w_query, w_key, w_value, w_out, block_ids, block_count, guidance):
    allowed = tile_table(block_ids, block_count)
    cond = one_branch(hidden_states[0], modulation[0], w_query, w_key, w_value, w_out, allowed)
    uncond = one_branch(hidden_states[1], modulation[1], w_query, w_key, w_value, w_out, allowed)
    return (uncond + guidance[0] * (cond - uncond)).astype(jnp.bfloat16)
```

```python
import functools
import math

import jax
import jax.numpy as jnp
from jax import lax
from jax.experimental import pallas as pl
from jax.experimental.pallas import tpu as pltpu
from jax.sharding import PartitionSpec as P

HD = 64
TILE = 128
MESH = pl.DeviceIdType.MESH
EXP_SCALE = 0.125 * math.log2(math.e)

NZ = 4
OWN_TILES = 3
SLAB = NZ * OWN_TILES
ROUNDS = 3
SLOTS = 12
TOK = OWN_TILES * TILE
GROUP = NZ * HD


def attention_kernel(
    x_hbm,
    mod_ref,
    wq_hbm,
    wk_hbm,
    wv_hbm,
    ids_ref,
    count_ref,
    out_ref,
    xbuf,
    hbuf,
    wbuf,
    stage,
    kv_0,
    kv_1,
    kv_2,
    qstage,
    qbuf,
    ret,
    back,
    scores,
    meta,
    meta_all,
    meta_smem,
    load_sem,
    z_send,
    z_recv,
    x_send,
    x_recv,
    q_send,
    q_recv,
    r_send,
    r_recv,
    m_send,
    m_recv,
    local_sem,
):
    seq = lax.axis_index("seq")
    guid = lax.axis_index("guid")
    tp = lax.axis_index("tp")
    px = seq // NZ
    pz = seq % NZ
    kv = (kv_0, kv_1, kv_2)

    def z_peer(dz):
        return (px * NZ + (pz + dz) % NZ, guid, tp)

    def x_peer(dx):
        return (((px + dx + NZ) % NZ) * NZ + pz, guid, tp)

    x_copy = pltpu.make_async_copy(x_hbm, xbuf, load_sem.at[9])
    x_copy.start()
    weights = {}
    order = [(kind, j) for j in range(ROUNDS) for kind in (1, 2)] + [(0, j) for j in range(ROUNDS)]
    for kind, j in order:
        source = (wq_hbm, wk_hbm, wv_hbm)[kind]
        slot = kind * ROUNDS + j
        copy = pltpu.make_async_copy(
            source.at[:, pl.ds(j * GROUP, GROUP)], wbuf.at[slot], load_sem.at[slot]
        )
        copy.start()
        weights[slot] = copy

    meta[...] = jnp.zeros_like(meta)
    meta[0:3, 0:SLOTS] = ids_ref[...]
    meta[3:4, 0:3] = count_ref[...]
    meta_all[pz] = meta[...]

    barrier = pltpu.get_barrier_semaphore()
    peers = [z_peer(dz) for dz in (1, 2, 3)] + [x_peer(dx) for dx in (1, -1)]
    for peer in peers:
        pl.semaphore_signal(barrier, inc=1, device_id=peer, device_id_type=MESH)
    pl.semaphore_wait(barrier, len(peers))

    def meta_copy(dz):
        return pltpu.make_async_remote_copy(
            src_ref=meta,
            dst_ref=meta_all.at[pz],
            send_sem=m_send.at[dz - 1],
            recv_sem=m_recv.at[dz - 1],
            device_id=z_peer(dz),
            device_id_type=MESH,
        )

    def z_copy(j, dz):
        return pltpu.make_async_remote_copy(
            src_ref=stage.at[j, (pz + dz) % NZ],
            dst_ref=kv[j].at[pl.ds(SLAB + pz * OWN_TILES, OWN_TILES)],
            send_sem=z_send.at[j, dz - 1],
            recv_sem=z_recv.at[j, dz - 1],
            device_id=z_peer(dz),
            device_id_type=MESH,
        )

    def own_copy(j):
        return pltpu.make_async_copy(
            stage.at[j, pz],
            kv[j].at[pl.ds(SLAB + pz * OWN_TILES, OWN_TILES)],
            local_sem.at[j],
        )

    def x_copy_of(j, dz, side):
        origin = (pz - dz + NZ) % NZ
        here = kv[j].at[pl.ds(SLAB + origin * OWN_TILES, OWN_TILES)]
        return pltpu.make_async_remote_copy(
            src_ref=stage.at[j, pz] if dz == 0 else here,
            dst_ref=kv[j].at[pl.ds(2 * SLAB * side + origin * OWN_TILES, OWN_TILES)],
            send_sem=x_send.at[j, dz, side],
            recv_sem=x_recv.at[j, dz, side],
            device_id=x_peer(1 - 2 * side),
            device_id_type=MESH,
        )

    def q_copy(j, dz):
        return pltpu.make_async_remote_copy(
            src_ref=qstage.at[j, (pz + dz) % NZ],
            dst_ref=qbuf.at[j, pz],
            send_sem=q_send.at[j, dz - 1],
            recv_sem=q_recv.at[j, dz - 1],
            device_id=z_peer(dz),
            device_id_type=MESH,
        )

    def r_copy(j, dz):
        return pltpu.make_async_remote_copy(
            src_ref=ret.at[j, (pz + dz) % NZ],
            dst_ref=back.at[j, pz],
            send_sem=r_send.at[j, dz - 1],
            recv_sem=r_recv.at[j, dz - 1],
            device_id=z_peer(dz),
            device_id_type=MESH,
        )

    for dz in (1, 2, 3):
        meta_copy(dz).start()

    x_copy.wait()
    rows = 16

    def norm_rows(i, carry):
        at = pl.ds(pl.multiple_of(i * rows, rows), rows)
        xf = xbuf[at, :].astype(jnp.float32)
        width = xf.shape[1]
        mean = jnp.sum(xf, axis=1, keepdims=True) * (1.0 / width)
        off = xf - mean
        var = jnp.sum(off * off, axis=1, keepdims=True) * (1.0 / width)
        scale = 1.0 / jnp.sqrt(var + 1e-05)
        hbuf[at, :] = (off * scale * (1.0 + mod_ref[1:2, :]) + mod_ref[0:1, :]).astype(
            jnp.bfloat16
        )
        return carry

    lax.fori_loop(0, TOK // rows, norm_rows, 0)

    def product(slot):
        weights[slot].wait()
        full = jnp.dot(hbuf[...], wbuf[slot], preferred_element_type=jnp.float32)
        return full.astype(jnp.bfloat16)

    def tiles_of(full):
        for i in range(OWN_TILES):
            part = full[i * TILE : (i + 1) * TILE, :]
            yield i, jnp.transpose(part).reshape(NZ, HD, TILE)

    def make_kv(j):
        for which in (0, 1):
            for i, part in tiles_of(product((1 + which) * ROUNDS + j)):
                stage[j, :, i, which] = part

    def forward(j):
        for dz in (1, 2, 3):
            z_copy(j, dz).wait_recv()
            for side in (0, 1):
                x_copy_of(j, dz, side).start()

    def make_q(j):
        for i, part in tiles_of(product(j)):
            qstage[j, :, i] = part
        for dz in (1, 2, 3):
            q_copy(j, dz).start()
        qbuf[j, pz] = qstage[j, pz]

    for j in range(ROUNDS):
        make_kv(j)
        for dz in (1, 2, 3):
            z_copy(j, dz).start()
        for side in (0, 1):
            x_copy_of(j, 0, side).start()
        own_copy(j).start()
    forward(0)
    make_q(0)
    forward(1)
    make_q(1)
    forward(2)
    make_q(2)

    for dz in (1, 2, 3):
        meta_copy(dz).wait_recv()
    meta_load = pltpu.make_async_copy(meta_all, meta_smem, local_sem.at[3])
    meta_load.start()
    meta_load.wait()

    first = (px - 1) * SLAB
    one_rows = jnp.ones((HD, TILE), jnp.bfloat16)
    zero_rows = jnp.zeros((HD, TILE), jnp.bfloat16)

    def attend(j, owner, i):
        q = jnp.transpose(qbuf[j, owner, i])
        top = None
        where = []
        for c in range(0, SLOTS, 2):
            spots = [
                jnp.clip(meta_smem[owner, i, c + e] - first, 0, 3 * SLAB - 1) for e in (0, 1)
            ]
            where.append(spots)
            pair = jnp.concatenate([kv[j][spot, 0] for spot in spots], axis=1)
            s = jnp.dot(q, pair, preferred_element_type=jnp.float32)
            scores[i, c // 2] = s
            top = s if top is None else jnp.maximum(top, s)
        top = jnp.max(top, axis=1, keepdims=True)
        live = meta_smem[owner, 3, i]
        acc = None
        for c in range(0, SLOTS, 2):
            p = jnp.exp2((scores[i, c // 2] - top) * EXP_SCALE).astype(jnp.bfloat16)
            sides = []
            for e in (0, 1):
                ok = (c + e) < live
                spot = where[c // 2][e]
                sides.append(
                    jnp.concatenate(
                        [
                            jnp.where(ok, kv[j][spot, 1], zero_rows),
                            jnp.where(ok, one_rows, zero_rows),
                        ],
                        axis=0,
                    )
                )
            values = jnp.concatenate(sides, axis=1)
            part = lax.dot_general(
                p, values, (((1,), (1,)), ((), ())), preferred_element_type=jnp.float32
            )
            acc = part if acc is None else acc + part
        both = jnp.transpose(acc)
        ret[j, owner, i] = (both[:HD] / both[HD:]).astype(jnp.bfloat16)

    for j in range(ROUNDS):
        own_copy(j).wait()
        for dz in (0, 1, 2, 3):
            for side in (0, 1):
                x_copy_of(j, dz, side).wait_recv()
        for dz in (1, 2, 3):
            q_copy(j, dz).wait_recv()

        def owner_step(step, carry, j=j):
            dz = (step + 1) % NZ
            owner = (pz + dz) % NZ
            for i in range(OWN_TILES):
                attend(j, owner, i)

            return carry

        lax.fori_loop(0, NZ, owner_step, 0)
        for dz in (1, 2, 3):
            r_copy(j, dz).start()
        back[j, pz] = ret[j, pz]

    for j in range(ROUNDS):
        for dz in (1, 2, 3):
            r_copy(j, dz).wait_recv()
        for i in range(OWN_TILES):
            part = back[j, :, i].reshape(GROUP, TILE)
            out_ref[pl.ds(i * TILE, TILE), pl.ds(j * GROUP, GROUP)] = jnp.transpose(part)

    for dz in (1, 2, 3):
        meta_copy(dz).wait_send()
    for j in range(ROUNDS):
        for dz in (1, 2, 3):
            z_copy(j, dz).wait_send()
            q_copy(j, dz).wait_send()
            r_copy(j, dz).wait_send()
        for dz in (0, 1, 2, 3):
            for side in (0, 1):
                x_copy_of(j, dz, side).wait_send()


def attention(states, modul, w_query, w_key, w_value, block_ids, block_count):
    width = states.shape[1]
    bf16 = jnp.bfloat16
    dma = pltpu.SemaphoreType.DMA
    any_spec = pl.BlockSpec(memory_space=pltpu.HBM)
    vmem_spec = pl.BlockSpec(memory_space=pltpu.VMEM)
    return pl.pallas_call(
        attention_kernel,
        out_shape=jax.ShapeDtypeStruct((TOK, ROUNDS * GROUP), bf16),
        in_specs=[any_spec, vmem_spec, any_spec, any_spec, any_spec, vmem_spec, vmem_spec],
        out_specs=vmem_spec,
        scratch_shapes=[
            pltpu.VMEM((TOK, width), bf16),
            pltpu.VMEM((TOK, width), bf16),
            pltpu.VMEM((3 * ROUNDS, width, GROUP), bf16),
            pltpu.VMEM((ROUNDS, NZ, OWN_TILES, 2, HD, TILE), bf16),
            pltpu.VMEM((3 * SLAB, 2, HD, TILE), bf16),
            pltpu.VMEM((3 * SLAB, 2, HD, TILE), bf16),
            pltpu.VMEM((3 * SLAB, 2, HD, TILE), bf16),
            pltpu.VMEM((ROUNDS, NZ, OWN_TILES, HD, TILE), bf16),
            pltpu.VMEM((ROUNDS, NZ, OWN_TILES, HD, TILE), bf16),
            pltpu.VMEM((ROUNDS, NZ, OWN_TILES, HD, TILE), bf16),
            pltpu.VMEM((ROUNDS, NZ, OWN_TILES, HD, TILE), bf16),
            pltpu.VMEM((OWN_TILES, SLOTS // 2, TILE, 2 * TILE), jnp.float32),
            pltpu.VMEM((8, 128), jnp.int32),
            pltpu.VMEM((NZ, 8, 128), jnp.int32),
            pltpu.SMEM((NZ, 8, 128), jnp.int32),
            dma((10,)),
            dma((ROUNDS, 3)),
            dma((ROUNDS, 3)),
            dma((ROUNDS, 4, 2)),
            dma((ROUNDS, 4, 2)),
            dma((ROUNDS, 3)),
            dma((ROUNDS, 3)),
            dma((ROUNDS, 3)),
            dma((ROUNDS, 3)),
            dma((3,)),
            dma((3,)),
            dma((4,)),
        ],
        compiler_params=pltpu.CompilerParams(
            collective_id=0, has_side_effects=True, vmem_limit_bytes=56 * 2**20
        ),
        name="attention",
    )(states, modul, w_query, w_key, w_value, block_ids, block_count)


def swapped(value, axis, distance):
    return lax.ppermute(value, axis, [(i, i ^ 1 << distance) for i in range(lax.axis_size(axis))])


def shards(
    hidden_states, modulation, w_query, w_key, w_value, w_out, block_ids, block_count, guidance
):
    states = hidden_states[0]
    modul = modulation[0]
    ntok = states.shape[0]
    attn = attention(
        states, modul, w_query, w_key, w_value, block_ids, block_count.reshape(1, -1)
    )
    xf = states.astype(jnp.float32)
    proj = jnp.dot(attn, w_out, preferred_element_type=jnp.float32)
    scale_now = guidance[0]
    branch = lax.axis_index("guid")
    tp_count = lax.axis_size("tp")
    tp_here = lax.axis_index("tp")
    model_width = states.shape[1]
    half = model_width // (2 * tp_count)

    def regroup(array):
        count = array.shape[0]
        return jnp.transpose(array.reshape(count, 2, tp_count, half), (0, 2, 1, 3)).reshape(
            count, model_width
        )

    shares = lax.psum_scatter(
        regroup(proj).astype(jnp.bfloat16), "tp", scatter_dimension=1, tiled=True
    ).astype(jnp.float32)
    x_part = lax.dynamic_slice_in_dim(regroup(xf), tp_here * 2 * half, 2 * half, 1)
    gate_part = lax.dynamic_slice_in_dim(
        regroup(modul[2][None, :]), tp_here * 2 * half, 2 * half, 1
    )
    block = (x_part + gate_part * shares).reshape(ntok, 2, half)
    own = lax.dynamic_slice_in_dim(block, branch, 1, 1)[:, 0]
    outgoing = lax.dynamic_slice_in_dim(block, 1 - branch, 1, 1)[:, 0]
    other = swapped(outgoing.astype(jnp.bfloat16), "guid", 0).astype(outgoing.dtype)
    cond = jnp.where(branch == 0, own, other)
    uncond = jnp.where(branch == 0, other, own)
    return (uncond + scale_now * (cond - uncond)).astype(jnp.bfloat16)


def solution(mesh):
    in_specs = (
        P("guid", "seq", None),
        P("guid", None, None),
        P(None, "tp"),
        P(None, "tp"),
        P(None, "tp"),
        P("tp", None),
        P("seq", None),
        P("seq"),
        P(),
    )
    out_specs = P("seq", ("guid", "tp"))
    return jax.shard_map(shards, mesh=mesh, in_specs=in_specs, out_specs=out_specs, check_vma=False)
```

```python
import functools
import math

import jax
import jax.numpy as jnp
from jax import lax
from jax.experimental import pallas as pl
from jax.experimental.pallas import tpu as pltpu
from jax.sharding import PartitionSpec as P

HD = 64
TILE = 128
MESH = pl.DeviceIdType.MESH
EXP_SCALE = 0.125 * math.log2(math.e)

NZ = 4
NY = 4
OWN_TILES = 3
SLAB = NZ * OWN_TILES
ROUNDS = 3
SLOTS = 12
TOK = OWN_TILES * TILE
GROUP = NZ * HD


def block_kernel(
    x_hbm,
    mod_ref,
    wq_hbm,
    wk_hbm,
    wv_hbm,
    wo_hbm,
    ids_ref,
    count_ref,
    guidance_ref,
    out_ref,
    xbuf,
    hbuf,
    wbuf,
    stage,
    kv_0,
    kv_1,
    kv_2,
    qstage,
    qbuf,
    ret,
    back,
    scores,
    wo,
    abuf,
    acc,
    xother,
    modother,
    meta,
    meta_all,
    meta_smem,
    load_sem,
    z_send,
    z_recv,
    x_send,
    x_recv,
    q_send,
    q_recv,
    r_send,
    r_recv,
    m_send,
    m_recv,
    w_send,
    w_recv,
    y_send,
    y_recv,
    c_send,
    c_recv,
    p_send,
    p_recv,
    local_sem,
):
    seq = lax.axis_index("seq")
    guid = lax.axis_index("guid")
    tp = lax.axis_index("tp")
    px = seq // NZ
    pz = seq % NZ
    kv = (kv_0, kv_1, kv_2)

    def z_peer(dz):
        return (px * NZ + (pz + dz) % NZ, guid, tp)

    def x_peer(dx):
        return (((px + dx + NZ) % NZ) * NZ + pz, guid, tp)

    def y_peer(dy):
        return (seq, guid, (tp + dy) % NY)

    partner = (seq, 1 - guid, tp)

    x_copy = pltpu.make_async_copy(x_hbm.at[0], xbuf, load_sem.at[9])
    x_copy.start()
    weights = {}
    order = [(kind, j) for j in range(ROUNDS) for kind in (1, 2)] + [(0, j) for j in range(ROUNDS)]
    for kind, j in order:
        source = (wq_hbm, wk_hbm, wv_hbm)[kind]
        slot = kind * ROUNDS + j
        copy = pltpu.make_async_copy(
            source.at[:, pl.ds(j * GROUP, GROUP)], wbuf.at[slot], load_sem.at[slot]
        )
        copy.start()
        weights[slot] = copy

    wo_own = pltpu.make_async_copy(
        wo_hbm.at[:, pl.ds(pl.multiple_of((guid * NY + tp) * TOK, TILE), TOK)],
        wo.at[tp],
        load_sem.at[10],
    )
    wo_own.start()

    meta[...] = jnp.zeros_like(meta)
    meta[0:3, 0:SLOTS] = ids_ref[...]
    meta[3:4, 0:3] = count_ref[...]
    meta_all[pz] = meta[...]

    barrier = pltpu.get_barrier_semaphore()
    peers = [z_peer(dz) for dz in (1, 2, 3)] + [x_peer(dx) for dx in (1, -1)]
    peers += [y_peer(dy) for dy in (1, 2, 3)] + [partner]
    for peer in peers:
        pl.semaphore_signal(barrier, inc=1, device_id=peer, device_id_type=MESH)
    pl.semaphore_wait(barrier, len(peers))

    def meta_copy(dz):
        return pltpu.make_async_remote_copy(
            src_ref=meta,
            dst_ref=meta_all.at[pz],
            send_sem=m_send.at[dz - 1],
            recv_sem=m_recv.at[dz - 1],
            device_id=z_peer(dz),
            device_id_type=MESH,
        )

    def z_copy(j, dz):
        return pltpu.make_async_remote_copy(
            src_ref=stage.at[j, (pz + dz) % NZ],
            dst_ref=kv[j].at[pl.ds(SLAB + pz * OWN_TILES, OWN_TILES)],
            send_sem=z_send.at[j, dz - 1],
            recv_sem=z_recv.at[j, dz - 1],
            device_id=z_peer(dz),
            device_id_type=MESH,
        )

    def own_copy(j):
        return pltpu.make_async_copy(
            stage.at[j, pz],
            kv[j].at[pl.ds(SLAB + pz * OWN_TILES, OWN_TILES)],
            local_sem.at[j],
        )

    def x_copy_of(j, dz, side):
        origin = (pz - dz + NZ) % NZ
        here = kv[j].at[pl.ds(SLAB + origin * OWN_TILES, OWN_TILES)]
        return pltpu.make_async_remote_copy(
            src_ref=stage.at[j, pz] if dz == 0 else here,
            dst_ref=kv[j].at[pl.ds(2 * SLAB * side + origin * OWN_TILES, OWN_TILES)],
            send_sem=x_send.at[j, dz, side],
            recv_sem=x_recv.at[j, dz, side],
            device_id=x_peer(1 - 2 * side),
            device_id_type=MESH,
        )

    def q_copy(j, dz):
        return pltpu.make_async_remote_copy(
            src_ref=qstage.at[j, (pz + dz) % NZ],
            dst_ref=qbuf.at[j, pz],
            send_sem=q_send.at[j, dz - 1],
            recv_sem=q_recv.at[j, dz - 1],
            device_id=z_peer(dz),
            device_id_type=MESH,
        )

    def r_copy(j, dz):
        return pltpu.make_async_remote_copy(
            src_ref=ret.at[j, (pz + dz) % NZ],
            dst_ref=back.at[j, pz],
            send_sem=r_send.at[j, dz - 1],
            recv_sem=r_recv.at[j, dz - 1],
            device_id=z_peer(dz),
            device_id_type=MESH,
        )

    def w_copy(dy):
        column = (guid * NY + (tp + dy) % NY) * TOK
        return pltpu.make_async_remote_copy(
            src_ref=wo_hbm.at[:, pl.ds(pl.multiple_of(column, TILE), TOK)],
            dst_ref=wo.at[tp],
            send_sem=w_send.at[dy - 1],
            recv_sem=w_recv.at[dy - 1],
            device_id=y_peer(dy),
            device_id_type=MESH,
        )

    def y_copy(j, dy):
        return pltpu.make_async_remote_copy(
            src_ref=abuf.at[guid, tp, j],
            dst_ref=abuf.at[guid, tp, j],
            send_sem=y_send.at[j, dy - 1],
            recv_sem=y_recv.at[j, dy - 1],
            device_id=y_peer(dy),
            device_id_type=MESH,
        )

    def c_copy(j, dy):
        origin = (tp - dy + NY) % NY
        return pltpu.make_async_remote_copy(
            src_ref=abuf.at[guid, origin, j],
            dst_ref=abuf.at[guid, origin, j],
            send_sem=c_send.at[j, dy],
            recv_sem=c_recv.at[j, dy],
            device_id=partner,
            device_id_type=MESH,
        )

    def p_copy(which):
        if which == 0:
            column = ((1 - guid) * NY + tp) * TOK
            source, target = xbuf.at[:, pl.ds(pl.multiple_of(column, TILE), TOK)], xother
        else:
            source, target = mod_ref, modother
        return pltpu.make_async_remote_copy(
            src_ref=source,
            dst_ref=target,
            send_sem=p_send.at[which],
            recv_sem=p_recv.at[which],
            device_id=partner,
            device_id_type=MESH,
        )

    for dz in (1, 2, 3):
        meta_copy(dz).start()
    for dy in (1, 3, 2):
        w_copy(dy).start()

    x_copy.wait()
    for which in (0, 1):
        p_copy(which).start()
    rows = 16

    def norm_rows(i, carry):
        at = pl.ds(pl.multiple_of(i * rows, rows), rows)
        xf = xbuf[at, :].astype(jnp.float32)
        width = xf.shape[1]
        mean = jnp.sum(xf, axis=1, keepdims=True) * (1.0 / width)
        off = xf - mean
        var = jnp.sum(off * off, axis=1, keepdims=True) * (1.0 / width)
        scale = 1.0 / jnp.sqrt(var + 1e-05)
        hbuf[at, :] = (off * scale * (1.0 + mod_ref[1]) + mod_ref[0]).astype(
            jnp.bfloat16
        )
        return carry

    lax.fori_loop(0, TOK // rows, norm_rows, 0)

    def product(slot):
        weights[slot].wait()
        full = jnp.dot(hbuf[...], wbuf[slot], preferred_element_type=jnp.float32)
        return full.astype(jnp.bfloat16)

    def tiles_of(full):
        for i in range(OWN_TILES):
            part = full[i * TILE : (i + 1) * TILE, :]
            yield i, jnp.transpose(part).reshape(NZ, HD, TILE)

    def make_kv(j):
        for which in (0, 1):
            for i, part in tiles_of(product((1 + which) * ROUNDS + j)):
                stage[j, :, i, which] = part

    def forward(j):
        for dz in (1, 2, 3):
            z_copy(j, dz).wait_recv()
            for side in (0, 1):
                x_copy_of(j, dz, side).start()

    def make_q(j):
        for i, part in tiles_of(product(j)):
            qstage[j, :, i] = part
        for dz in (1, 2, 3):
            q_copy(j, dz).start()
        qbuf[j, pz] = qstage[j, pz]

    for j in range(ROUNDS):
        make_kv(j)
        for dz in (1, 2, 3):
            z_copy(j, dz).start()
        for side in (0, 1):
            x_copy_of(j, 0, side).start()
        own_copy(j).start()
    forward(0)
    make_q(0)
    forward(1)
    make_q(1)
    forward(2)
    make_q(2)

    for dz in (1, 2, 3):
        meta_copy(dz).wait_recv()
    meta_load = pltpu.make_async_copy(meta_all, meta_smem, local_sem.at[3])
    meta_load.start()
    meta_load.wait()

    first = (px - 1) * SLAB
    one_rows = jnp.ones((HD, TILE), jnp.bfloat16)
    zero_rows = jnp.zeros((HD, TILE), jnp.bfloat16)

    def attend(j, owner, i):
        q = jnp.transpose(qbuf[j, owner, i])
        top = None
        where = []
        for c in range(0, SLOTS, 2):
            spots = [
                jnp.clip(meta_smem[owner, i, c + e] - first, 0, 3 * SLAB - 1) for e in (0, 1)
            ]
            where.append(spots)
            pair = jnp.concatenate([kv[j][spot, 0] for spot in spots], axis=1)
            s = jnp.dot(q, pair, preferred_element_type=jnp.float32)
            scores[i, c // 2] = s
            top = s if top is None else jnp.maximum(top, s)
        top = jnp.max(top, axis=1, keepdims=True)
        live = meta_smem[owner, 3, i]
        acc = None
        for c in range(0, SLOTS, 2):
            p = jnp.exp2((scores[i, c // 2] - top) * EXP_SCALE).astype(jnp.bfloat16)
            sides = []
            for e in (0, 1):
                ok = (c + e) < live
                spot = where[c // 2][e]
                sides.append(
                    jnp.concatenate(
                        [
                            jnp.where(ok, kv[j][spot, 1], zero_rows),
                            jnp.where(ok, one_rows, zero_rows),
                        ],
                        axis=0,
                    )
                )
            values = jnp.concatenate(sides, axis=1)
            part = lax.dot_general(
                p, values, (((1,), (1,)), ((), ())), preferred_element_type=jnp.float32
            )
            acc = part if acc is None else acc + part
        both = jnp.transpose(acc)
        ret[j, owner, i] = (both[:HD] / both[HD:]).astype(jnp.bfloat16)

    def attention_round(j):
        own_copy(j).wait()
        for dz in (0, 1, 2, 3):
            for side in (0, 1):
                x_copy_of(j, dz, side).wait_recv()
        for dz in (1, 2, 3):
            q_copy(j, dz).wait_recv()

        def owner_step(step, carry):
            owner = (pz + step + 1) % NZ
            for i in range(OWN_TILES):
                attend(j, owner, i)
            return carry

        lax.fori_loop(0, NZ, owner_step, 0)
        for dz in (1, 2, 3):
            r_copy(j, dz).start()
        back[j, pz] = ret[j, pz]

    def gather(j):
        for dz in (1, 2, 3):
            r_copy(j, dz).wait_recv()
        for i in range(OWN_TILES):
            part = back[j, :, i].reshape(GROUP, TILE)
            abuf[guid, tp, j, pl.ds(i * TILE, TILE), :] = jnp.transpose(part)
        for dy in (1, 3, 2):
            y_copy(j, dy).start()
        c_copy(j, 0).start()

    def spread(j):
        for dy in (1, 3, 2):
            y_copy(j, dy).wait_recv()
            c_copy(j, dy).start()

    def product_of(branch, js):
        def one(y, carry):
            total = None
            for j in js:
                part = jnp.dot(
                    abuf[branch, y, j],
                    wo[y, pl.ds(j * GROUP, GROUP), :],
                    preferred_element_type=jnp.float32,
                )
                total = part if total is None else total + part
            acc[branch] += total
            return carry

        lax.fori_loop(0, NY, one, 0)

    attention_round(0)
    attention_round(1)
    gather(0)
    attention_round(2)
    gather(1)
    spread(0)
    acc[...] = jnp.zeros_like(acc)
    wo_own.wait()
    for dy in (1, 2, 3):
        w_copy(dy).wait_recv()
    gather(2)
    spread(1)
    for j in (0, 1):
        for dy in (0, 1, 2, 3):
            c_copy(j, dy).wait_recv()
    for branch in (0, 1):
        product_of(branch, (0, 1))
    spread(2)
    product_of(guid, (2,))
    for dy in (0, 1, 2, 3):
        c_copy(2, dy).wait_recv()
    product_of(1 - guid, (2,))

    for which in (0, 1):
        p_copy(which).wait_recv()
    column = pl.ds(pl.multiple_of((guid * NY + tp) * TOK, TILE), TOK)
    strength = guidance_ref[0]
    gate_own = mod_ref[2, :, column]
    gate_other = modother[2, :, column]
    own = xbuf[:, column].astype(jnp.float32) + gate_own * acc[guid]
    other = xother[...].astype(jnp.float32) + gate_other * acc[1 - guid]
    cond = jnp.where(guid == 0, own, other)
    uncond = jnp.where(guid == 0, other, own)
    out_ref[...] = (uncond + strength * (cond - uncond)).astype(jnp.bfloat16)

    for which in (0, 1):
        p_copy(which).wait_send()
    for dy in (1, 2, 3):
        w_copy(dy).wait_send()
    for dz in (1, 2, 3):
        meta_copy(dz).wait_send()
    for j in range(ROUNDS):
        for dy in (1, 2, 3):
            y_copy(j, dy).wait_send()
        for dy in (0, 1, 2, 3):
            c_copy(j, dy).wait_send()
        for dz in (1, 2, 3):
            z_copy(j, dz).wait_send()
            q_copy(j, dz).wait_send()
            r_copy(j, dz).wait_send()
        for dz in (0, 1, 2, 3):
            for side in (0, 1):
                x_copy_of(j, dz, side).wait_send()


def shards(
    hidden_states, modulation, w_query, w_key, w_value, w_out, block_ids, block_count, guidance
):
    width = hidden_states.shape[2]
    bf16 = jnp.bfloat16
    dma = pltpu.SemaphoreType.DMA
    any_spec = pl.BlockSpec(memory_space=pltpu.HBM)
    vmem_spec = pl.BlockSpec(memory_space=pltpu.VMEM)
    smem_spec = pl.BlockSpec(memory_space=pltpu.SMEM)
    per_round = pltpu.VMEM((ROUNDS, NZ, OWN_TILES, HD, TILE), bf16)
    pairs = []
    for shape in (
        (ROUNDS, 3),
        (ROUNDS, 4, 2),
        (ROUNDS, 3),
        (ROUNDS, 3),
        (3,),
        (3,),
        (ROUNDS, 3),
        (ROUNDS, 4),
        (2,),
    ):
        pairs += [dma(shape), dma(shape)]
    return pl.pallas_call(
        block_kernel,
        out_shape=jax.ShapeDtypeStruct((TOK, TOK), bf16),
        in_specs=[any_spec, vmem_spec]
        + [any_spec] * 4
        + [vmem_spec, vmem_spec, smem_spec],
        out_specs=vmem_spec,
        scratch_shapes=[
            pltpu.VMEM((TOK, width), bf16),
            pltpu.VMEM((TOK, width), bf16),
            pltpu.VMEM((3 * ROUNDS, width, GROUP), bf16),
            pltpu.VMEM((ROUNDS, NZ, OWN_TILES, 2, HD, TILE), bf16),
            pltpu.VMEM((3 * SLAB, 2, HD, TILE), bf16),
            pltpu.VMEM((3 * SLAB, 2, HD, TILE), bf16),
            pltpu.VMEM((3 * SLAB, 2, HD, TILE), bf16),
            per_round,
            per_round,
            per_round,
            per_round,
            pltpu.VMEM((OWN_TILES, SLOTS // 2, TILE, 2 * TILE), jnp.float32),
            pltpu.VMEM((NY, ROUNDS * GROUP, TOK), bf16),
            pltpu.VMEM((2, NY, ROUNDS, TOK, GROUP), bf16),
            pltpu.VMEM((2, TOK, TOK), jnp.float32),
            pltpu.VMEM((TOK, TOK), bf16),
            pltpu.VMEM((3, 1, width), jnp.float32),
            pltpu.VMEM((8, 128), jnp.int32),
            pltpu.VMEM((NZ, 8, 128), jnp.int32),
            pltpu.SMEM((NZ, 8, 128), jnp.int32),
            dma((11,)),
            *pairs,
            dma((4,)),
        ],
        compiler_params=pltpu.CompilerParams(
            collective_id=0, has_side_effects=True, vmem_limit_bytes=60 * 2**20
        ),
        name="block",
    )(
        hidden_states,
        jnp.transpose(modulation, (1, 0, 2)),
        w_query,
        w_key,
        w_value,
        w_out,
        block_ids,
        block_count.reshape(1, -1),
        guidance,
    )


def solution(mesh):
    in_specs = (
        P("guid", "seq", None),
        P("guid", None, None),
        P(None, "tp"),
        P(None, "tp"),
        P(None, "tp"),
        P("tp", None),
        P("seq", None),
        P("seq"),
        P(),
    )
    out_specs = P("seq", ("guid", "tp"))
    return jax.shard_map(shards, mesh=mesh, in_specs=in_specs, out_specs=out_specs, check_vma=False)
```

```python
import functools

import jax
import jax.numpy as jnp
from jax import lax
from jax.experimental import pallas as pl
from jax.experimental.pallas import tpu as pltpu
from jax.sharding import PartitionSpec as P

HD = 64
TILE = 128
MESH = pl.DeviceIdType.MESH

NZ = 4
NY = 4
OWN_TILES = 3
SLAB = NZ * OWN_TILES
ROUNDS = 3
SLOTS = 12
TOK = OWN_TILES * TILE
GROUP = NZ * HD


def block_kernel(
    x_hbm,
    mod_ref,
    wq_hbm,
    wk_hbm,
    wv_hbm,
    wo_hbm,
    ids_ref,
    count_ref,
    guidance_ref,
    out_ref,
    xbuf,
    hbuf,
    wbuf,
    stage,
    kv_0,
    kv_1,
    kv_2,
    qstage,
    qbuf,
    ret,
    back,
    scores,
    wo,
    abuf,
    acc,
    xother,
    modother,
    meta,
    meta_all,
    meta_smem,
    load_sem,
    z_send,
    z_recv,
    x_send,
    x_recv,
    q_send,
    q_recv,
    r_send,
    r_recv,
    m_send,
    m_recv,
    w_send,
    w_recv,
    y_send,
    y_recv,
    c_send,
    c_recv,
    p_send,
    p_recv,
    f_send,
    f_recv,
    local_sem,
):
    seq = lax.axis_index("seq")
    guid = lax.axis_index("guid")
    tp = lax.axis_index("tp")
    px = seq // NZ
    pz = seq % NZ
    kv = (kv_0, kv_1, kv_2)

    def z_peer(dz):
        return (px * NZ + (pz + dz) % NZ, guid, tp)

    def x_peer(dx):
        return (((px + dx + NZ) % NZ) * NZ + pz, guid, tp)

    def y_peer(dy):
        return (seq, guid, (tp + dy) % NY)

    partner = (seq, 1 - guid, tp)

    x_copy = pltpu.make_async_copy(x_hbm.at[0], xbuf, load_sem.at[9])
    x_copy.start()
    weights = {}
    order = [(kind, j) for j in range(ROUNDS) for kind in (1, 2)] + [(0, j) for j in range(ROUNDS)]
    for kind, j in order:
        source = (wq_hbm, wk_hbm, wv_hbm)[kind]
        slot = kind * ROUNDS + j
        copy = pltpu.make_async_copy(
            source.at[:, pl.ds(j * GROUP, GROUP)], wbuf.at[slot], load_sem.at[slot]
        )
        copy.start()
        weights[slot] = copy

    wo_own = pltpu.make_async_copy(
        wo_hbm.at[:, pl.ds(pl.multiple_of((guid * NY + tp) * TOK, TILE), TOK)],
        wo.at[tp],
        load_sem.at[10],
    )
    wo_own.start()

    meta[...] = jnp.zeros_like(meta)
    meta[0:3, 0:SLOTS] = ids_ref[...]
    meta[3:4, 0:3] = count_ref[...]
    meta_all[pz] = meta[...]

    barrier = pltpu.get_barrier_semaphore()
    peers = [z_peer(dz) for dz in (1, 2, 3)] + [x_peer(dx) for dx in (1, -1)]
    peers += [y_peer(dy) for dy in (1, 2, 3)] + [partner]
    for peer in peers:
        pl.semaphore_signal(barrier, inc=1, device_id=peer, device_id_type=MESH)
    pl.semaphore_wait(barrier, len(peers))

    def meta_copy(dz):
        return pltpu.make_async_remote_copy(
            src_ref=meta,
            dst_ref=meta_all.at[pz],
            send_sem=m_send.at[dz - 1],
            recv_sem=m_recv.at[dz - 1],
            device_id=z_peer(dz),
            device_id_type=MESH,
        )

    def z_copy(j, dz):
        return pltpu.make_async_remote_copy(
            src_ref=stage.at[j, (pz + dz) % NZ],
            dst_ref=kv[j].at[pl.ds(SLAB + pz * OWN_TILES, OWN_TILES)],
            send_sem=z_send.at[j, dz - 1],
            recv_sem=z_recv.at[j, dz - 1],
            device_id=z_peer(dz),
            device_id_type=MESH,
        )

    def own_copy(j):
        return pltpu.make_async_copy(
            stage.at[j, pz],
            kv[j].at[pl.ds(SLAB + pz * OWN_TILES, OWN_TILES)],
            local_sem.at[j],
        )

    def x_copy_of(j, dz, side):
        origin = (pz - dz + NZ) % NZ
        here = kv[j].at[pl.ds(SLAB + origin * OWN_TILES, OWN_TILES)]
        return pltpu.make_async_remote_copy(
            src_ref=stage.at[j, pz] if dz == 0 else here,
            dst_ref=kv[j].at[pl.ds(2 * SLAB * side + origin * OWN_TILES, OWN_TILES)],
            send_sem=x_send.at[j, dz, side],
            recv_sem=x_recv.at[j, dz, side],
            device_id=x_peer(1 - 2 * side),
            device_id_type=MESH,
        )

    def q_copy(j, dz):
        return pltpu.make_async_remote_copy(
            src_ref=qstage.at[j, (pz + dz) % NZ],
            dst_ref=qbuf.at[j, pz],
            send_sem=q_send.at[j, dz - 1],
            recv_sem=q_recv.at[j, dz - 1],
            device_id=z_peer(dz),
            device_id_type=MESH,
        )

    def r_copy(j, dz):
        return pltpu.make_async_remote_copy(
            src_ref=ret.at[j, (pz + dz) % NZ],
            dst_ref=back.at[j, pz],
            send_sem=r_send.at[j, dz - 1],
            recv_sem=r_recv.at[j, dz - 1],
            device_id=z_peer(dz),
            device_id_type=MESH,
        )

    def w_copy(dy):
        column = (guid * NY + (tp + dy) % NY) * TOK
        return pltpu.make_async_remote_copy(
            src_ref=wo_hbm.at[:, pl.ds(pl.multiple_of(column, TILE), TOK)],
            dst_ref=wo.at[tp],
            send_sem=w_send.at[dy - 1],
            recv_sem=w_recv.at[dy - 1],
            device_id=y_peer(dy),
            device_id_type=MESH,
        )

    def y_copy(j, dy):
        return pltpu.make_async_remote_copy(
            src_ref=abuf.at[guid, tp, j],
            dst_ref=abuf.at[guid, tp, j],
            send_sem=y_send.at[j, dy - 1],
            recv_sem=y_recv.at[j, dy - 1],
            device_id=y_peer(dy),
            device_id_type=MESH,
        )

    def f_copy(j, way):
        step = 1 - 2 * way
        half = abuf.at[guid, (tp - step + NY) % NY, j, pl.ds(way * (TOK // 2), TOK // 2)]
        return pltpu.make_async_remote_copy(
            src_ref=half,
            dst_ref=half,
            send_sem=f_send.at[j, way],
            recv_sem=f_recv.at[j, way],
            device_id=y_peer((step + NY) % NY),
            device_id_type=MESH,
        )

    def c_copy(j, dy):
        origin = (tp - dy + NY) % NY
        return pltpu.make_async_remote_copy(
            src_ref=abuf.at[guid, origin, j],
            dst_ref=abuf.at[guid, origin, j],
            send_sem=c_send.at[j, dy],
            recv_sem=c_recv.at[j, dy],
            device_id=partner,
            device_id_type=MESH,
        )

    def p_copy(which):
        if which == 0:
            column = ((1 - guid) * NY + tp) * TOK
            source, target = xbuf.at[:, pl.ds(pl.multiple_of(column, TILE), TOK)], xother
        else:
            source, target = mod_ref, modother
        return pltpu.make_async_remote_copy(
            src_ref=source,
            dst_ref=target,
            send_sem=p_send.at[which],
            recv_sem=p_recv.at[which],
            device_id=partner,
            device_id_type=MESH,
        )

    for dz in (1, 2, 3):
        meta_copy(dz).start()
    for dy in (1, 3, 2):
        w_copy(dy).start()

    x_copy.wait()
    for which in (0, 1):
        p_copy(which).start()
    rows = 16

    def norm_rows(i, carry):
        at = pl.ds(pl.multiple_of(i * rows, rows), rows)
        xf = xbuf[at, :].astype(jnp.float32)
        width = xf.shape[1]
        mean = jnp.sum(xf, axis=1, keepdims=True) * (1.0 / width)
        off = xf - mean
        var = jnp.sum(off * off, axis=1, keepdims=True) * (1.0 / width)
        scale = 1.0 / jnp.sqrt(var + 1e-05)
        hbuf[at, :] = (off * scale * (1.0 + mod_ref[1]) + mod_ref[0]).astype(
            jnp.bfloat16
        )
        return carry

    lax.fori_loop(0, TOK // rows, norm_rows, 0, unroll=8)

    def product(slot):
        weights[slot].wait()
        full = jnp.dot(hbuf[...], wbuf[slot], preferred_element_type=jnp.float32)
        return full.astype(jnp.bfloat16)

    def tiles_of(full):
        for i in range(OWN_TILES):
            part = full[i * TILE : (i + 1) * TILE, :]
            yield i, jnp.transpose(part).reshape(NZ, HD, TILE)

    def make_kv(j):
        for which in (0, 1):
            for i, part in tiles_of(product((1 + which) * ROUNDS + j)):
                stage[j, :, i, which] = part

    def forward(j):
        for dz in (1, 2, 3):
            z_copy(j, dz).wait_recv()
            for side in (0, 1):
                x_copy_of(j, dz, side).start()

    def make_q(j):
        for i, part in tiles_of(product(j)):
            qstage[j, :, i] = part
        for dz in (1, 2, 3):
            q_copy(j, dz).start()
        qbuf[j, pz] = qstage[j, pz]

    for j in range(ROUNDS):
        make_kv(j)
        for dz in (1, 2, 3):
            z_copy(j, dz).start()
        for side in (0, 1):
            x_copy_of(j, 0, side).start()
        own_copy(j).start()
    forward(0)
    make_q(0)
    forward(1)
    make_q(1)
    forward(2)
    make_q(2)

    for dz in (1, 2, 3):
        meta_copy(dz).wait_recv()
    meta_load = pltpu.make_async_copy(meta_all, meta_smem, local_sem.at[3])
    meta_load.start()
    meta_load.wait()

    first = (px - 1) * SLAB
    one_rows = jnp.ones((HD, TILE), jnp.bfloat16)
    zero_rows = jnp.zeros((HD, TILE), jnp.bfloat16)

    def attend(j, owner, i, spot_of):
        q = jnp.transpose(qbuf[j, owner, i]) * jnp.asarray(0.125, jnp.bfloat16)
        top = None
        where = []
        for c in range(0, SLOTS, 2):
            spots = [
                jnp.clip(meta_smem[owner, i, c + e] - first, 0, 3 * SLAB - 1) for e in (0, 1)
            ]
            where.append(spots)
            pair = jnp.concatenate([kv[j][spot, 0] for spot in spots], axis=1)
            s = jnp.dot(q, pair, preferred_element_type=jnp.float32)
            scores[spot_of, c // 2] = s
            top = s if top is None else jnp.maximum(top, s)
        top = jnp.max(top, axis=1, keepdims=True)
        live = meta_smem[owner, 3, i]
        acc = None
        for c in range(0, SLOTS, 2):
            p = jnp.exp(scores[spot_of, c // 2] - top).astype(jnp.bfloat16)
            sides = []
            for e in (0, 1):
                ok = (c + e) < live
                spot = where[c // 2][e]
                sides.append(
                    jnp.concatenate(
                        [
                            jnp.where(ok, kv[j][spot, 1], zero_rows),
                            jnp.where(ok, one_rows, zero_rows),
                        ],
                        axis=0,
                    )
                )
            values = jnp.concatenate(sides, axis=1)
            part = lax.dot_general(
                p, values, (((1,), (1,)), ((), ())), preferred_element_type=jnp.float32
            )
            acc = part if acc is None else acc + part
        both = jnp.transpose(acc)
        ret[j, owner, i] = (both[:HD] / both[HD:]).astype(jnp.bfloat16)

    def attention_round(j):
        own_copy(j).wait()
        for dz in (0, 1, 2, 3):
            for side in (0, 1):
                x_copy_of(j, dz, side).wait_recv()
        for dz in (1, 2, 3):
            q_copy(j, dz).wait_recv()

        for step in range(NZ):
            owner = (pz + step + 1) % NZ
            for i in range(OWN_TILES):
                attend(j, owner, i, step * OWN_TILES + i)
        for dz in (1, 2, 3):
            r_copy(j, dz).start()
        back[j, pz] = ret[j, pz]

    def gather(j):
        for dz in (1, 2, 3):
            r_copy(j, dz).wait_recv()
        for i in range(OWN_TILES):
            part = back[j, :, i].reshape(GROUP, TILE)
            abuf[guid, tp, j, pl.ds(i * TILE, TILE), :] = jnp.transpose(part)
        for dy in (1, 3):
            y_copy(j, dy).start()
        c_copy(j, 0).start()

    def spread(j):
        for dy in (1, 3):
            y_copy(j, dy).wait_recv()
            f_copy(j, dy // 2).start()
            c_copy(j, dy).start()

    def spread_far(j):
        for way in (0, 1):
            f_copy(j, way).wait_recv()
        c_copy(j, 2).start()

    def product_of(branch, js):
        def one(y, carry):
            total = None
            for j in js:
                part = jnp.dot(
                    abuf[branch, y, j],
                    wo[y, pl.ds(j * GROUP, GROUP), :],
                    preferred_element_type=jnp.float32,
                )
                total = part if total is None else total + part
            acc[branch] += total
            return carry

        lax.fori_loop(0, NY, one, 0)

    def arrived(j):
        for dy in (0, 1, 2, 3):
            c_copy(j, dy).wait_recv()

    acc[...] = jnp.zeros_like(acc)
    attention_round(0)
    gather(0)
    attention_round(1)
    spread(0)
    gather(1)
    attention_round(2)
    spread_far(0)
    spread(1)
    wo_own.wait()
    for dy in (1, 2, 3):
        w_copy(dy).wait_recv()
    arrived(0)
    for branch in (0, 1):
        product_of(branch, (0,))
    gather(2)
    spread_far(1)
    arrived(1)
    for branch in (0, 1):
        product_of(branch, (1,))
    spread(2)
    spread_far(2)
    product_of(guid, (2,))
    arrived(2)
    product_of(1 - guid, (2,))

    for which in (0, 1):
        p_copy(which).wait_recv()
    column = pl.ds(pl.multiple_of((guid * NY + tp) * TOK, TILE), TOK)
    strength = guidance_ref[...]
    gate_own = mod_ref[2, :, column]
    gate_other = modother[2, :, column]
    own = xbuf[:, column].astype(jnp.float32) + gate_own * acc[guid]
    other = xother[...].astype(jnp.float32) + gate_other * acc[1 - guid]
    cond = jnp.where(guid == 0, own, other)
    uncond = jnp.where(guid == 0, other, own)
    out_ref[...] = (uncond + strength * (cond - uncond)).astype(jnp.bfloat16)

    for which in (0, 1):
        p_copy(which).wait_send()
    for dy in (1, 2, 3):
        w_copy(dy).wait_send()
    for dz in (1, 2, 3):
        meta_copy(dz).wait_send()
    for j in range(ROUNDS):
        for dy in (1, 3):
            y_copy(j, dy).wait_send()
        for way in (0, 1):
            f_copy(j, way).wait_send()
        for dy in (0, 1, 2, 3):
            c_copy(j, dy).wait_send()
        for dz in (1, 2, 3):
            z_copy(j, dz).wait_send()
            q_copy(j, dz).wait_send()
            r_copy(j, dz).wait_send()
        for dz in (0, 1, 2, 3):
            for side in (0, 1):
                x_copy_of(j, dz, side).wait_send()


def shards(
    hidden_states, modulation, w_query, w_key, w_value, w_out, block_ids, block_count, guidance
):
    width = hidden_states.shape[2]
    bf16 = jnp.bfloat16
    dma = pltpu.SemaphoreType.DMA
    any_spec = pl.BlockSpec(memory_space=pltpu.HBM)
    vmem_spec = pl.BlockSpec(memory_space=pltpu.VMEM)
    per_round = pltpu.VMEM((ROUNDS, NZ, OWN_TILES, HD, TILE), bf16)
    pairs = []
    for shape in (
        (ROUNDS, 3),
        (ROUNDS, 4, 2),
        (ROUNDS, 3),
        (ROUNDS, 3),
        (3,),
        (3,),
        (ROUNDS, 3),
        (ROUNDS, 4),
        (2,),
        (ROUNDS, 2),
    ):
        pairs += [dma(shape), dma(shape)]
    return pl.pallas_call(
        block_kernel,
        out_shape=jax.ShapeDtypeStruct((TOK, TOK), bf16),
        in_specs=[any_spec, vmem_spec]
        + [any_spec] * 4
        + [vmem_spec] * 3,
        out_specs=vmem_spec,
        scratch_shapes=[
            pltpu.VMEM((TOK, width), bf16),
            pltpu.VMEM((TOK, width), bf16),
            pltpu.VMEM((3 * ROUNDS, width, GROUP), bf16),
            pltpu.VMEM((ROUNDS, NZ, OWN_TILES, 2, HD, TILE), bf16),
            pltpu.VMEM((3 * SLAB, 2, HD, TILE), bf16),
            pltpu.VMEM((3 * SLAB, 2, HD, TILE), bf16),
            pltpu.VMEM((3 * SLAB, 2, HD, TILE), bf16),
            per_round,
            per_round,
            per_round,
            per_round,
            pltpu.VMEM((SLAB, SLOTS // 2, TILE, 2 * TILE), jnp.float32),
            pltpu.VMEM((NY, ROUNDS * GROUP, TOK), bf16),
            pltpu.VMEM((2, NY, ROUNDS, TOK, GROUP), bf16),
            pltpu.VMEM((2, TOK, TOK), jnp.float32),
            pltpu.VMEM((TOK, TOK), bf16),
            pltpu.VMEM((3, 1, width), jnp.float32),
            pltpu.VMEM((8, 128), jnp.int32),
            pltpu.VMEM((NZ, 8, 128), jnp.int32),
            pltpu.SMEM((NZ, 8, 128), jnp.int32),
            dma((11,)),
            *pairs,
            dma((4,)),
        ],
        compiler_params=pltpu.CompilerParams(
            collective_id=0, has_side_effects=True, vmem_limit_bytes=60 * 2**20
        ),
        name="block",
    )(
        hidden_states,
        jnp.transpose(modulation, (1, 0, 2)),
        w_query,
        w_key,
        w_value,
        w_out,
        block_ids,
        block_count.reshape(1, -1),
        guidance.reshape(1, 1),
    )


def solution(mesh):
    in_specs = (
        P("guid", "seq", None),
        P("guid", None, None),
        P(None, "tp"),
        P(None, "tp"),
        P(None, "tp"),
        P("tp", None),
        P("seq", None),
        P("seq"),
        P(),
    )
    out_specs = P("seq", ("guid", "tp"))
    return jax.shard_map(shards, mesh=mesh, in_specs=in_specs, out_specs=out_specs, check_vma=False)
```

```python
import functools

import jax
import jax.numpy as jnp
from jax import lax
from jax.experimental import pallas as pl
from jax.experimental.pallas import tpu as pltpu
from jax.sharding import PartitionSpec as P

HD = 64
TILE = 128
MESH = pl.DeviceIdType.MESH

NZ = 4
NY = 4
OWN_TILES = 3
SLAB = NZ * OWN_TILES
ROUNDS = 3
SLOTS = 12
TOK = OWN_TILES * TILE
GROUP = NZ * HD
PIECES = ((0, 0, 3), (1, 0, 3), (2, 0, 1), (2, 1, 1), (2, 2, 1))


def block_kernel(
    x_hbm,
    mod_ref,
    wq_hbm,
    wk_hbm,
    wv_hbm,
    wo_hbm,
    ids_ref,
    count_ref,
    guidance_ref,
    out_ref,
    xbuf,
    hbuf,
    wbuf,
    stage,
    kv_0,
    kv_1,
    kv_2,
    qstage,
    qbuf,
    ret,
    back,
    scores,
    wo,
    abuf,
    acc,
    xother,
    modother,
    meta,
    meta_all,
    meta_smem,
    load_sem,
    z_send,
    z_recv,
    x_send,
    x_recv,
    q_send,
    q_recv,
    r_send,
    r_recv,
    m_send,
    m_recv,
    w_send,
    w_recv,
    y_send,
    y_recv,
    c_send,
    c_recv,
    p_send,
    p_recv,
    f_send,
    f_recv,
    local_sem,
):
    seq = lax.axis_index("seq")
    guid = lax.axis_index("guid")
    tp = lax.axis_index("tp")
    px = seq // NZ
    pz = seq % NZ
    kv = (kv_0, kv_1, kv_2)

    def z_peer(dz):
        return (px * NZ + (pz + dz) % NZ, guid, tp)

    def x_peer(dx):
        return (((px + dx + NZ) % NZ) * NZ + pz, guid, tp)

    def y_peer(dy):
        return (seq, guid, (tp + dy) % NY)

    partner = (seq, 1 - guid, tp)

    def x_load(i):
        rows = pl.ds(i * TILE, TILE)
        return pltpu.make_async_copy(x_hbm.at[0, rows], xbuf.at[rows], load_sem.at[9 + i])

    def w_load(kind, j):
        source = (wq_hbm, wk_hbm, wv_hbm)[kind]
        slot = kind * ROUNDS + j
        return pltpu.make_async_copy(
            source.at[:, pl.ds(j * GROUP, GROUP)], wbuf.at[slot], load_sem.at[slot]
        )

    for i in range(OWN_TILES):
        x_load(i).start()
    w_load(1, 0).start()
    w_load(2, 0).start()

    wo_own = pltpu.make_async_copy(
        wo_hbm.at[:, pl.ds(pl.multiple_of((guid * NY + tp) * TOK, TILE), TOK)],
        wo.at[tp],
        load_sem.at[12],
    )

    meta[...] = jnp.zeros_like(meta)
    meta[0:3, 0:SLOTS] = ids_ref[...]
    meta[3:4, 0:3] = count_ref[...]
    meta_all[pz] = meta[...]

    barrier = pltpu.get_barrier_semaphore()
    peers = [z_peer(dz) for dz in (1, 2, 3)] + [x_peer(dx) for dx in (1, -1)]
    peers += [y_peer(dy) for dy in (1, 2, 3)] + [partner]
    for peer in peers:
        pl.semaphore_signal(barrier, inc=1, device_id=peer, device_id_type=MESH)
    pl.semaphore_wait(barrier, len(peers))

    def meta_copy(dz):
        return pltpu.make_async_remote_copy(
            src_ref=meta,
            dst_ref=meta_all.at[pz],
            send_sem=m_send.at[dz - 1],
            recv_sem=m_recv.at[dz - 1],
            device_id=z_peer(dz),
            device_id_type=MESH,
        )

    def z_copy(j, dz):
        return pltpu.make_async_remote_copy(
            src_ref=stage.at[j, (pz + dz) % NZ],
            dst_ref=kv[j].at[pl.ds(SLAB + pz * OWN_TILES, OWN_TILES)],
            send_sem=z_send.at[j, dz - 1],
            recv_sem=z_recv.at[j, dz - 1],
            device_id=z_peer(dz),
            device_id_type=MESH,
        )

    def own_copy(j):
        return pltpu.make_async_copy(
            stage.at[j, pz],
            kv[j].at[pl.ds(SLAB + pz * OWN_TILES, OWN_TILES)],
            local_sem.at[j],
        )

    def x_copy_of(j, dz, side):
        origin = (pz - dz + NZ) % NZ
        here = kv[j].at[pl.ds(SLAB + origin * OWN_TILES, OWN_TILES)]
        return pltpu.make_async_remote_copy(
            src_ref=stage.at[j, pz] if dz == 0 else here,
            dst_ref=kv[j].at[pl.ds(2 * SLAB * side + origin * OWN_TILES, OWN_TILES)],
            send_sem=x_send.at[j, dz, side],
            recv_sem=x_recv.at[j, dz, side],
            device_id=x_peer(1 - 2 * side),
            device_id_type=MESH,
        )

    def q_copy(j, dz):
        return pltpu.make_async_remote_copy(
            src_ref=qstage.at[j, (pz + dz) % NZ],
            dst_ref=qbuf.at[j, pz],
            send_sem=q_send.at[j, dz - 1],
            recv_sem=q_recv.at[j, dz - 1],
            device_id=z_peer(dz),
            device_id_type=MESH,
        )

    def r_copy(p, dz):
        j, first_tile, count = PIECES[p]
        tiles = pl.ds(first_tile, count)
        return pltpu.make_async_remote_copy(
            src_ref=ret.at[j, (pz + dz) % NZ, tiles],
            dst_ref=back.at[j, pz, tiles],
            send_sem=r_send.at[p, dz - 1],
            recv_sem=r_recv.at[p, dz - 1],
            device_id=z_peer(dz),
            device_id_type=MESH,
        )

    def w_copy(dy):
        column = (guid * NY + (tp + dy) % NY) * TOK
        return pltpu.make_async_remote_copy(
            src_ref=wo_hbm.at[:, pl.ds(pl.multiple_of(column, TILE), TOK)],
            dst_ref=wo.at[tp],
            send_sem=w_send.at[dy - 1],
            recv_sem=w_recv.at[dy - 1],
            device_id=y_peer(dy),
            device_id_type=MESH,
        )

    def y_copy(p, dy):
        j, first_tile, count = PIECES[p]
        part = abuf.at[guid, tp, j, pl.ds(first_tile * TILE, count * TILE)]
        return pltpu.make_async_remote_copy(
            src_ref=part,
            dst_ref=part,
            send_sem=y_send.at[p, dy // 2],
            recv_sem=y_recv.at[p, dy // 2],
            device_id=y_peer(dy),
            device_id_type=MESH,
        )

    def f_copy(p, way):
        j, first_tile, count = PIECES[p]
        step = 1 - 2 * way
        size = count * TILE // 2
        half = abuf.at[
            guid, (tp - step + NY) % NY, j, pl.ds(first_tile * TILE + way * size, size)
        ]
        return pltpu.make_async_remote_copy(
            src_ref=half,
            dst_ref=half,
            send_sem=f_send.at[p, way],
            recv_sem=f_recv.at[p, way],
            device_id=y_peer((step + NY) % NY),
            device_id_type=MESH,
        )

    def c_copy(p, dy):
        j, first_tile, count = PIECES[p]
        origin = (tp - dy + NY) % NY
        part = abuf.at[guid, origin, j, pl.ds(first_tile * TILE, count * TILE)]
        return pltpu.make_async_remote_copy(
            src_ref=part,
            dst_ref=part,
            send_sem=c_send.at[p, dy],
            recv_sem=c_recv.at[p, dy],
            device_id=partner,
            device_id_type=MESH,
        )

    def p_copy(which):
        if which == 0:
            column = ((1 - guid) * NY + tp) * TOK
            source, target = xbuf.at[:, pl.ds(pl.multiple_of(column, TILE), TOK)], xother
        else:
            source, target = mod_ref, modother
        return pltpu.make_async_remote_copy(
            src_ref=source,
            dst_ref=target,
            send_sem=p_send.at[which],
            recv_sem=p_recv.at[which],
            device_id=partner,
            device_id_type=MESH,
        )

    rows = 16
    gain = 1.0 + mod_ref[1]
    for i in range(OWN_TILES):
        x_load(i).wait()
        if i == 0:
            w_load(1, 1).start()
            w_load(2, 1).start()
        if i == 1:
            w_load(1, 2).start()
            w_load(2, 2).start()

        def norm_rows(n, carry, i=i):
            at = pl.ds(pl.multiple_of(i * TILE + n * rows, rows), rows)
            xf = xbuf[at, :].astype(jnp.float32)
            width = xf.shape[1]
            mean = jnp.sum(xf, axis=1, keepdims=True) * (1.0 / width)
            off = xf - mean
            var = jnp.sum(off * off, axis=1, keepdims=True) * (1.0 / width)
            scale = 1.0 / jnp.sqrt(var + 1e-05)
            hbuf[at, :] = (off * scale * gain + mod_ref[0]).astype(jnp.bfloat16)
            return carry

        lax.fori_loop(0, TILE // rows, norm_rows, 0, unroll=8)
    for j in range(ROUNDS):
        w_load(0, j).start()

    def product(slot):
        w_load(slot // ROUNDS, slot % ROUNDS).wait()
        full = jnp.dot(hbuf[...], wbuf[slot], preferred_element_type=jnp.float32)
        return full.astype(jnp.bfloat16)

    def tiles_of(full):
        for i in range(OWN_TILES):
            part = full[i * TILE : (i + 1) * TILE, :]
            yield i, jnp.transpose(part).reshape(NZ, HD, TILE)

    def make_kv(j):
        for which in (0, 1):
            for i, part in tiles_of(product((1 + which) * ROUNDS + j)):
                stage[j, :, i, which] = part

    def forward(j):
        for dz in (1, 3, 2):
            z_copy(j, dz).wait_recv()
            for side in (0, 1):
                x_copy_of(j, dz, side).start()

    def make_q(j):
        for i, part in tiles_of(product(j)):
            qstage[j, :, i] = part
        qbuf[j, pz] = qstage[j, pz]

    def send_z(j):
        for dz in (1, 3, 2):
            z_copy(j, dz).start()

    def send_q(j):
        for dz in (1, 3, 2):
            q_copy(j, dz).start()

    for j in range(ROUNDS):
        make_kv(j)
        if j == 0:
            send_z(0)
        for side in (0, 1):
            x_copy_of(j, 0, side).start()
        own_copy(j).start()
        if j == 0:
            for dz in (1, 2, 3):
                meta_copy(dz).start()
            for which in (0, 1):
                p_copy(which).start()
            for dy in (1, 3, 2):
                w_copy(dy).start()
    wo_own.start()
    make_q(0)
    forward(0)
    send_z(1)
    send_q(0)
    make_q(1)
    make_q(2)
    forward(1)
    send_z(2)
    send_q(1)
    send_q(2)

    for dz in (1, 2, 3):
        meta_copy(dz).wait_recv()
    meta_load = pltpu.make_async_copy(meta_all, meta_smem, local_sem.at[3])
    meta_load.start()
    meta_load.wait()

    first = (px - 1) * SLAB
    one_rows = jnp.ones((HD, TILE), jnp.bfloat16)
    zero_rows = jnp.zeros((HD, TILE), jnp.bfloat16)

    def attend(j, owner, i, spot_of):
        q = jnp.transpose(qbuf[j, owner, i]) * jnp.asarray(0.125, jnp.bfloat16)
        top = None
        where = []
        for c in range(0, SLOTS, 2):
            spots = [
                jnp.clip(meta_smem[owner, i, c + e] - first, 0, 3 * SLAB - 1) for e in (0, 1)
            ]
            where.append(spots)
            pair = jnp.concatenate([kv[j][spot, 0] for spot in spots], axis=1)
            s = jnp.dot(q, pair, preferred_element_type=jnp.float32)
            scores[spot_of, c // 2] = s
            top = s if top is None else jnp.maximum(top, s)
        top = jnp.max(top, axis=1, keepdims=True)
        live = meta_smem[owner, 3, i]
        acc = None
        for c in range(0, SLOTS, 2):
            p = jnp.exp(scores[spot_of, c // 2] - top).astype(jnp.bfloat16)
            sides = []
            for e in (0, 1):
                ok = (c + e) < live
                spot = where[c // 2][e]
                sides.append(
                    jnp.concatenate(
                        [
                            jnp.where(ok, kv[j][spot, 1], zero_rows),
                            jnp.where(ok, one_rows, zero_rows),
                        ],
                        axis=0,
                    )
                )
            values = jnp.concatenate(sides, axis=1)
            part = lax.dot_general(
                p, values, (((1,), (1,)), ((), ())), preferred_element_type=jnp.float32
            )
            acc = part if acc is None else acc + part
        both = jnp.transpose(acc)
        ret[j, owner, i] = (both[:HD] / both[HD:]).astype(jnp.bfloat16)

    def ready(j):
        own_copy(j).wait()
        for dz in (0, 1, 3, 2):
            for side in (0, 1):
                x_copy_of(j, dz, side).wait_recv()
        for dz in (1, 3, 2):
            q_copy(j, dz).wait_recv()

    def attention_piece(p):
        j, first_tile, count = PIECES[p]
        for step in range(NZ):
            owner = (pz + step + 1) % NZ
            for i in range(first_tile, first_tile + count):
                attend(j, owner, i, step * OWN_TILES + i)
        for dz in (1, 3, 2):
            r_copy(p, dz).start()
        tiles = pl.ds(first_tile, count)
        back[j, pz, tiles] = ret[j, pz, tiles]

    def gather(p):
        j, first_tile, count = PIECES[p]
        for dz in (1, 3, 2):
            r_copy(p, dz).wait_recv()
        for i in range(first_tile, first_tile + count):
            part = back[j, :, i].reshape(GROUP, TILE)
            abuf[guid, tp, j, pl.ds(i * TILE, TILE), :] = jnp.transpose(part)
        for dy in (1, 3):
            y_copy(p, dy).start()
        c_copy(p, 0).start()

    def spread(p):
        for dy in (1, 3):
            y_copy(p, dy).wait_recv()
            f_copy(p, dy // 2).start()
            c_copy(p, dy).start()

    def spread_far(p):
        for way in (0, 1):
            f_copy(p, way).wait_recv()
        c_copy(p, 2).start()

    def arrived(p):
        for dy in (0, 1, 3, 2):
            c_copy(p, dy).wait_recv()

    def part_of(branch, p, y):
        j, first_tile, count = PIECES[p]
        return jnp.dot(
            abuf[branch, y, j, pl.ds(first_tile * TILE, count * TILE), :],
            wo[y, pl.ds(j * GROUP, GROUP), :],
            preferred_element_type=jnp.float32,
        )

    def accumulate(p):
        arrived(p)
        for branch in (0, 1):

            def one(y, carry, branch=branch):
                acc[branch] += part_of(branch, p, y)
                return carry

            lax.fori_loop(0, NY, one, 0)

    column = pl.ds(pl.multiple_of((guid * NY + tp) * TOK, TILE), TOK)

    def finish(p):
        j, first_tile, count = PIECES[p]
        at = pl.ds(first_tile * TILE, count * TILE)
        strength = guidance_ref[...]

        def total(branch):
            summed = acc[branch, at, :]
            for y in range(NY):
                summed = summed + part_of(branch, p, y)
            return summed

        own = xbuf[at, column].astype(jnp.float32) + mod_ref[2, :, column] * total(guid)
        arrived(p)
        other = xother[at, :].astype(jnp.float32) + modother[2, :, column] * total(1 - guid)
        cond = jnp.where(guid == 0, own, other)
        uncond = jnp.where(guid == 0, other, own)
        out_ref[at, :] = (uncond + strength * (cond - uncond)).astype(jnp.bfloat16)

    acc[...] = jnp.zeros_like(acc)
    ready(0)
    attention_piece(0)
    forward(2)
    gather(0)
    ready(1)
    attention_piece(1)
    spread(0)
    gather(1)
    ready(2)
    attention_piece(2)
    spread_far(0)
    spread(1)
    attention_piece(3)
    gather(2)
    spread_far(1)
    attention_piece(4)
    gather(3)
    spread(2)
    wo_own.wait()
    for dy in (1, 2, 3):
        w_copy(dy).wait_recv()
    accumulate(0)
    gather(4)
    spread(3)
    spread_far(2)
    accumulate(1)
    spread(4)
    spread_far(3)
    for which in (0, 1):
        p_copy(which).wait_recv()
    finish(2)
    spread_far(4)
    finish(3)
    finish(4)

    for which in (0, 1):
        p_copy(which).wait_send()
    for dy in (1, 2, 3):
        w_copy(dy).wait_send()
    for dz in (1, 2, 3):
        meta_copy(dz).wait_send()
    for j in range(ROUNDS):
        for dz in (1, 2, 3):
            z_copy(j, dz).wait_send()
            q_copy(j, dz).wait_send()
        for dz in (0, 1, 2, 3):
            for side in (0, 1):
                x_copy_of(j, dz, side).wait_send()
    for p in range(len(PIECES)):
        for dz in (1, 2, 3):
            r_copy(p, dz).wait_send()
        for dy in (1, 3):
            y_copy(p, dy).wait_send()
        for way in (0, 1):
            f_copy(p, way).wait_send()
        for dy in (0, 1, 2, 3):
            c_copy(p, dy).wait_send()


def shards(
    hidden_states, modulation, w_query, w_key, w_value, w_out, block_ids, block_count, guidance
):
    width = hidden_states.shape[2]
    bf16 = jnp.bfloat16
    dma = pltpu.SemaphoreType.DMA
    any_spec = pl.BlockSpec(memory_space=pltpu.HBM)
    vmem_spec = pl.BlockSpec(memory_space=pltpu.VMEM)
    per_round = pltpu.VMEM((ROUNDS, NZ, OWN_TILES, HD, TILE), bf16)
    pairs = []
    count = len(PIECES)
    for shape in (
        (ROUNDS, 3),
        (ROUNDS, 4, 2),
        (ROUNDS, 3),
        (count, 3),
        (3,),
        (3,),
        (count, 2),
        (count, 4),
        (2,),
        (count, 2),
    ):
        pairs += [dma(shape), dma(shape)]
    return pl.pallas_call(
        block_kernel,
        out_shape=jax.ShapeDtypeStruct((TOK, TOK), bf16),
        in_specs=[any_spec, vmem_spec]
        + [any_spec] * 4
        + [vmem_spec] * 3,
        out_specs=vmem_spec,
        scratch_shapes=[
            pltpu.VMEM((TOK, width), bf16),
            pltpu.VMEM((TOK, width), bf16),
            pltpu.VMEM((3 * ROUNDS, width, GROUP), bf16),
            pltpu.VMEM((ROUNDS, NZ, OWN_TILES, 2, HD, TILE), bf16),
            pltpu.VMEM((3 * SLAB, 2, HD, TILE), bf16),
            pltpu.VMEM((3 * SLAB, 2, HD, TILE), bf16),
            pltpu.VMEM((3 * SLAB, 2, HD, TILE), bf16),
            per_round,
            per_round,
            per_round,
            per_round,
            pltpu.VMEM((SLAB, SLOTS // 2, TILE, 2 * TILE), jnp.float32),
            pltpu.VMEM((NY, ROUNDS * GROUP, TOK), bf16),
            pltpu.VMEM((2, NY, ROUNDS, TOK, GROUP), bf16),
            pltpu.VMEM((2, TOK, TOK), jnp.float32),
            pltpu.VMEM((TOK, TOK), bf16),
            pltpu.VMEM((3, 1, width), jnp.float32),
            pltpu.VMEM((8, 128), jnp.int32),
            pltpu.VMEM((NZ, 8, 128), jnp.int32),
            pltpu.SMEM((NZ, 8, 128), jnp.int32),
            dma((13,)),
            *pairs,
            dma((4,)),
        ],
        compiler_params=pltpu.CompilerParams(
            collective_id=0, has_side_effects=True, vmem_limit_bytes=60 * 2**20
        ),
        name="block",
    )(
        hidden_states,
        jnp.transpose(modulation, (1, 0, 2)),
        w_query,
        w_key,
        w_value,
        w_out,
        block_ids,
        block_count.reshape(1, -1),
        guidance.reshape(1, 1),
    )


def solution(mesh):
    in_specs = (
        P("guid", "seq", None),
        P("guid", None, None),
        P(None, "tp"),
        P(None, "tp"),
        P(None, "tp"),
        P("tp", None),
        P("seq", None),
        P("seq"),
        P(),
    )
    out_specs = P("seq", ("guid", "tp"))
    return jax.shard_map(shards, mesh=mesh, in_specs=in_specs, out_specs=out_specs, check_vma=False)
```

```python
import functools

import jax
import jax.numpy as jnp
from jax import lax
from jax.experimental import pallas as pl
from jax.experimental.pallas import tpu as pltpu
from jax.sharding import PartitionSpec as P

HD = 64
TILE = 128
MESH = pl.DeviceIdType.MESH

NZ = 4
NY = 4
OWN_TILES = 3
SLAB = NZ * OWN_TILES
ROUNDS = 3
SLOTS = 12
TOK = OWN_TILES * TILE
GROUP = NZ * HD
PIECES = ((0, 0, 3), (1, 0, 3), (2, 0, 1), (2, 1, 1), (2, 2, 1))


def block_kernel(
    x_hbm,
    mod_ref,
    wq_hbm,
    wk_hbm,
    wv_hbm,
    wo_hbm,
    ids_ref,
    count_ref,
    guidance_ref,
    out_ref,
    xbuf,
    hbuf,
    wbuf,
    stage,
    kv_0,
    kv_1,
    kv_2,
    qstage,
    qbuf,
    ret,
    back,
    scores,
    wo,
    abuf,
    acc,
    xother,
    modother,
    meta,
    meta_all,
    meta_smem,
    load_sem,
    z_send,
    z_recv,
    x_send,
    x_recv,
    q_send,
    q_recv,
    r_send,
    r_recv,
    m_send,
    m_recv,
    w_send,
    w_recv,
    y_send,
    y_recv,
    c_send,
    c_recv,
    p_send,
    p_recv,
    f_send,
    f_recv,
    local_sem,
):
    seq = lax.axis_index("seq")
    guid = lax.axis_index("guid")
    tp = lax.axis_index("tp")
    px = seq // NZ
    pz = seq % NZ
    kv = (kv_0, kv_1, kv_2)

    def z_peer(dz):
        return (px * NZ + (pz + dz) % NZ, guid, tp)

    def x_peer(dx):
        return (((px + dx + NZ) % NZ) * NZ + pz, guid, tp)

    def y_peer(dy):
        return (seq, guid, (tp + dy) % NY)

    partner = (seq, 1 - guid, tp)

    def x_load(i):
        rows = pl.ds(i * TILE, TILE)
        return pltpu.make_async_copy(x_hbm.at[0, rows], xbuf.at[rows], load_sem.at[9 + i])

    def w_load(kind, j):
        source = (wq_hbm, wk_hbm, wv_hbm)[kind]
        slot = kind * ROUNDS + j
        return pltpu.make_async_copy(
            source.at[:, pl.ds(j * GROUP, GROUP)], wbuf.at[slot], load_sem.at[slot]
        )

    for i in range(OWN_TILES):
        x_load(i).start()
    w_load(1, 0).start()
    w_load(2, 0).start()

    wo_own = pltpu.make_async_copy(
        wo_hbm.at[:, pl.ds(pl.multiple_of((guid * NY + tp) * TOK, TILE), TOK)],
        wo.at[tp],
        load_sem.at[12],
    )

    meta[...] = jnp.zeros_like(meta)
    meta[0:3, 0:SLOTS] = ids_ref[...]
    meta[3:4, 0:3] = count_ref[...]
    meta_all[pz] = meta[...]

    barrier = pltpu.get_barrier_semaphore()
    peers = [z_peer(dz) for dz in (1, 2, 3)] + [x_peer(dx) for dx in (1, -1)]
    peers += [y_peer(dy) for dy in (1, 2, 3)] + [partner]
    for peer in peers:
        pl.semaphore_signal(barrier, inc=1, device_id=peer, device_id_type=MESH)
    pl.semaphore_wait(barrier, len(peers))

    def meta_copy(dz):
        return pltpu.make_async_remote_copy(
            src_ref=meta,
            dst_ref=meta_all.at[pz],
            send_sem=m_send.at[dz - 1],
            recv_sem=m_recv.at[dz - 1],
            device_id=z_peer(dz),
            device_id_type=MESH,
        )

    def z_copy(j, dz):
        return pltpu.make_async_remote_copy(
            src_ref=stage.at[j, (pz + dz) % NZ],
            dst_ref=kv[j].at[pl.ds(SLAB + (NZ - dz) * OWN_TILES, OWN_TILES)],
            send_sem=z_send.at[j, dz - 1],
            recv_sem=z_recv.at[j, dz - 1],
            device_id=z_peer(dz),
            device_id_type=MESH,
        )

    def own_copy(j):
        return pltpu.make_async_copy(
            stage.at[j, pz], kv[j].at[pl.ds(SLAB, OWN_TILES)], local_sem.at[j]
        )

    def x_copy_of(j, rest, side):
        first_slot, count = (OWN_TILES, SLAB - OWN_TILES) if rest else (0, OWN_TILES)
        return pltpu.make_async_remote_copy(
            src_ref=kv[j].at[pl.ds(SLAB + first_slot, count)] if rest else stage.at[j, pz],
            dst_ref=kv[j].at[pl.ds(2 * SLAB * side + first_slot, count)],
            send_sem=x_send.at[j, rest, side],
            recv_sem=x_recv.at[j, rest, side],
            device_id=x_peer(1 - 2 * side),
            device_id_type=MESH,
        )

    def q_copy(j, dz):
        return pltpu.make_async_remote_copy(
            src_ref=qstage.at[j, (pz + dz) % NZ],
            dst_ref=qbuf.at[j, pz],
            send_sem=q_send.at[j, dz - 1],
            recv_sem=q_recv.at[j, dz - 1],
            device_id=z_peer(dz),
            device_id_type=MESH,
        )

    def r_copy(p, dz):
        j, first_tile, count = PIECES[p]
        tiles = pl.ds(first_tile, count)
        return pltpu.make_async_remote_copy(
            src_ref=ret.at[j, (pz + dz) % NZ, tiles],
            dst_ref=back.at[j, pz, tiles],
            send_sem=r_send.at[p, dz - 1],
            recv_sem=r_recv.at[p, dz - 1],
            device_id=z_peer(dz),
            device_id_type=MESH,
        )

    def w_copy(dy):
        column = (guid * NY + (tp + dy) % NY) * TOK
        return pltpu.make_async_remote_copy(
            src_ref=wo_hbm.at[:, pl.ds(pl.multiple_of(column, TILE), TOK)],
            dst_ref=wo.at[tp],
            send_sem=w_send.at[dy - 1],
            recv_sem=w_recv.at[dy - 1],
            device_id=y_peer(dy),
            device_id_type=MESH,
        )

    def y_copy(p, dy):
        j, first_tile, count = PIECES[p]
        part = abuf.at[guid, tp, j, pl.ds(first_tile * TILE, count * TILE)]
        return pltpu.make_async_remote_copy(
            src_ref=part,
            dst_ref=part,
            send_sem=y_send.at[p, dy - 1],
            recv_sem=y_recv.at[p, dy - 1],
            device_id=y_peer(dy),
            device_id_type=MESH,
        )

    def f_copy(p, way):
        j, first_tile, count = PIECES[p]
        step = 1 - 2 * way
        size = count * TILE // 2
        half = abuf.at[
            guid, (tp - step + NY) % NY, j, pl.ds(first_tile * TILE + way * size, size)
        ]
        return pltpu.make_async_remote_copy(
            src_ref=half,
            dst_ref=half,
            send_sem=f_send.at[p, way],
            recv_sem=f_recv.at[p, way],
            device_id=y_peer((step + NY) % NY),
            device_id_type=MESH,
        )

    def c_copy(p, dy):
        j, first_tile, count = PIECES[p]
        origin = (tp - dy + NY) % NY
        part = abuf.at[guid, origin, j, pl.ds(first_tile * TILE, count * TILE)]
        return pltpu.make_async_remote_copy(
            src_ref=part,
            dst_ref=part,
            send_sem=c_send.at[p, dy],
            recv_sem=c_recv.at[p, dy],
            device_id=partner,
            device_id_type=MESH,
        )

    def p_copy(which):
        if which == 0:
            column = ((1 - guid) * NY + tp) * TOK
            source, target = xbuf.at[:, pl.ds(pl.multiple_of(column, TILE), TOK)], xother
        else:
            source, target = mod_ref, modother
        return pltpu.make_async_remote_copy(
            src_ref=source,
            dst_ref=target,
            send_sem=p_send.at[which],
            recv_sem=p_recv.at[which],
            device_id=partner,
            device_id_type=MESH,
        )

    rows = 16
    gain = 1.0 + mod_ref[1]
    for i in range(OWN_TILES):
        x_load(i).wait()
        if i == 0:
            w_load(1, 1).start()
            w_load(2, 1).start()
        if i == 1:
            w_load(1, 2).start()
            w_load(2, 2).start()

        def norm_rows(n, carry, i=i):
            at = pl.ds(pl.multiple_of(i * TILE + n * rows, rows), rows)
            xf = xbuf[at, :].astype(jnp.float32)
            width = xf.shape[1]
            mean = jnp.sum(xf, axis=1, keepdims=True) * (1.0 / width)
            off = xf - mean
            var = jnp.sum(off * off, axis=1, keepdims=True) * (1.0 / width)
            scale = 1.0 / jnp.sqrt(var + 1e-05)
            hbuf[at, :] = (off * scale * gain + mod_ref[0]).astype(jnp.bfloat16)
            return carry

        lax.fori_loop(0, TILE // rows, norm_rows, 0, unroll=8)
    for j in range(ROUNDS):
        w_load(0, j).start()

    def product(slot):
        w_load(slot // ROUNDS, slot % ROUNDS).wait()
        full = jnp.dot(hbuf[...], wbuf[slot], preferred_element_type=jnp.float32)
        return full.astype(jnp.bfloat16)

    def tiles_of(full):
        for i in range(OWN_TILES):
            part = full[i * TILE : (i + 1) * TILE, :]
            yield i, jnp.transpose(part).reshape(NZ, HD, TILE)

    def make_kv(j):
        for which in (0, 1):
            for i, part in tiles_of(product((1 + which) * ROUNDS + j)):
                stage[j, :, i, which] = part

    def z_arrived(j):
        for dz in (1, 3, 2):
            z_copy(j, dz).wait_recv()

    def forward(j):
        for side in (0, 1):
            x_copy_of(j, 1, side).start()

    def make_q(j):
        for i, part in tiles_of(product(j)):
            qstage[j, :, i] = part
        qbuf[j, pz] = qstage[j, pz]

    def send_z(j):
        for dz in (1, 3, 2):
            z_copy(j, dz).start()

    def send_q(j):
        for dz in (1, 3, 2):
            q_copy(j, dz).start()

    for j in range(ROUNDS):
        make_kv(j)
        if j == 0:
            send_z(0)
        for side in (0, 1):
            x_copy_of(j, 0, side).start()
        own_copy(j).start()
        if j == 0:
            for dz in (1, 2, 3):
                meta_copy(dz).start()
            for which in (0, 1):
                p_copy(which).start()
            for dy in (1, 3, 2):
                w_copy(dy).start()
    wo_own.start()
    make_q(0)
    z_arrived(0)
    send_z(1)
    send_q(0)
    forward(0)
    make_q(1)
    make_q(2)
    z_arrived(1)
    send_z(2)
    send_q(1)
    send_q(2)
    forward(1)

    for dz in (1, 2, 3):
        meta_copy(dz).wait_recv()
    listed = meta_all[...]
    block = (listed * 171) >> 9
    slab = jnp.clip((block >> 2) - px + 1, 0, 2)
    slot = slab * SLAB + ((block - pz) & 3) * OWN_TILES + (listed - 3 * block)
    slot = jnp.clip(slot, 0, 3 * SLAB - 1)
    row = lax.broadcasted_iota(jnp.int32, listed.shape, 1)
    meta_all[...] = jnp.where(row == 3, listed, slot)
    meta_load = pltpu.make_async_copy(meta_all, meta_smem, local_sem.at[3])
    meta_load.start()
    meta_load.wait()

    one_rows = jnp.ones((HD, TILE), jnp.bfloat16)
    zero_rows = jnp.zeros((HD, TILE), jnp.bfloat16)

    def attend(j, owner, i, spot_of):
        q = jnp.transpose(qbuf[j, owner, i]) * jnp.asarray(0.125, jnp.bfloat16)
        top = None
        where = []
        for c in range(0, SLOTS, 2):
            spots = [meta_smem[owner, i, c + e] for e in (0, 1)]
            where.append(spots)
            pair = jnp.concatenate([kv[j][spot, 0] for spot in spots], axis=1)
            s = jnp.dot(q, pair, preferred_element_type=jnp.float32)
            scores[spot_of, c // 2] = s
            top = s if top is None else jnp.maximum(top, s)
        top = jnp.max(top, axis=1, keepdims=True)
        live = meta_smem[owner, 3, i]
        acc = None
        for c in range(0, SLOTS, 2):
            p = jnp.exp(scores[spot_of, c // 2] - top).astype(jnp.bfloat16)
            sides = []
            for e in (0, 1):
                ok = (c + e) < live
                spot = where[c // 2][e]
                sides.append(
                    jnp.concatenate(
                        [
                            jnp.where(ok, kv[j][spot, 1], zero_rows),
                            jnp.where(ok, one_rows, zero_rows),
                        ],
                        axis=0,
                    )
                )
            values = jnp.concatenate(sides, axis=1)
            part = lax.dot_general(
                p, values, (((1,), (1,)), ((), ())), preferred_element_type=jnp.float32
            )
            acc = part if acc is None else acc + part
        both = jnp.transpose(acc)
        ret[j, owner, i] = (both[:HD] / both[HD:]).astype(jnp.bfloat16)

    def ready(j):
        own_copy(j).wait()
        for rest in (0, 1):
            for side in (0, 1):
                x_copy_of(j, rest, side).wait_recv()
        for dz in (1, 3, 2):
            q_copy(j, dz).wait_recv()

    def attention_piece(p):
        j, first_tile, count = PIECES[p]
        for step in range(NZ):
            owner = (pz + step + 1) % NZ
            for i in range(first_tile, first_tile + count):
                attend(j, owner, i, step * OWN_TILES + i)
        for dz in (1, 3, 2):
            r_copy(p, dz).start()
        tiles = pl.ds(first_tile, count)
        back[j, pz, tiles] = ret[j, pz, tiles]

    def direct(p):
        return PIECES[p][0] == ROUNDS - 1

    def gather(p):
        j, first_tile, count = PIECES[p]
        for dz in (1, 3, 2):
            r_copy(p, dz).wait_recv()
        for i in range(first_tile, first_tile + count):
            part = back[j, :, i].reshape(GROUP, TILE)
            abuf[guid, tp, j, pl.ds(i * TILE, TILE), :] = jnp.transpose(part)
        for dy in (1, 3, 2) if direct(p) else (1, 3):
            y_copy(p, dy).start()
        c_copy(p, 0).start()

    def spread(p):
        for dy in (1, 3):
            y_copy(p, dy).wait_recv()
            if not direct(p):
                f_copy(p, dy // 2).start()
            c_copy(p, dy).start()

    def spread_far(p):
        if direct(p):
            y_copy(p, 2).wait_recv()
        else:
            for way in (0, 1):
                f_copy(p, way).wait_recv()
        c_copy(p, 2).start()

    def arrived(p):
        for dy in (0, 1, 3, 2):
            c_copy(p, dy).wait_recv()

    def part_of(branch, p, y):
        j, first_tile, count = PIECES[p]
        return jnp.dot(
            abuf[branch, y, j, pl.ds(first_tile * TILE, count * TILE), :],
            wo[y, pl.ds(j * GROUP, GROUP), :],
            preferred_element_type=jnp.float32,
        )

    def accumulate(p):
        arrived(p)
        for branch in (0, 1):

            def one(y, carry, branch=branch):
                acc[branch] += part_of(branch, p, y)
                return carry

            lax.fori_loop(0, NY, one, 0)

    column = pl.ds(pl.multiple_of((guid * NY + tp) * TOK, TILE), TOK)

    def finish(p):
        j, first_tile, count = PIECES[p]
        at = pl.ds(first_tile * TILE, count * TILE)
        strength = guidance_ref[...]

        def total(branch):
            summed = acc[branch, at, :]
            for y in range(NY):
                summed = summed + part_of(branch, p, y)
            return summed

        own = xbuf[at, column].astype(jnp.float32) + mod_ref[2, :, column] * total(guid)
        arrived(p)
        other = xother[at, :].astype(jnp.float32) + modother[2, :, column] * total(1 - guid)
        cond = jnp.where(guid == 0, own, other)
        uncond = jnp.where(guid == 0, other, own)
        out_ref[at, :] = (uncond + strength * (cond - uncond)).astype(jnp.bfloat16)

    def sent_kv(j):
        for dz in (1, 2, 3):
            z_copy(j, dz).wait_send()
            q_copy(j, dz).wait_send()
        for rest in (0, 1):
            for side in (0, 1):
                x_copy_of(j, rest, side).wait_send()

    def sent_piece(p):
        for dz in (1, 2, 3):
            r_copy(p, dz).wait_send()
        for dy in (1, 3, 2) if direct(p) else (1, 3):
            y_copy(p, dy).wait_send()
        if not direct(p):
            for way in (0, 1):
                f_copy(p, way).wait_send()
        for dy in (0, 1, 2, 3):
            c_copy(p, dy).wait_send()

    acc[...] = jnp.zeros_like(acc)
    ready(0)
    attention_piece(0)
    z_arrived(2)
    forward(2)
    gather(0)
    ready(1)
    attention_piece(1)
    spread(0)
    gather(1)
    for which in (0, 1):
        p_copy(which).wait_recv()
        p_copy(which).wait_send()
    for dz in (1, 2, 3):
        meta_copy(dz).wait_send()
    sent_kv(0)
    ready(2)
    attention_piece(2)
    spread_far(0)
    spread(1)
    attention_piece(3)
    gather(2)
    spread_far(1)
    attention_piece(4)
    gather(3)
    wo_own.wait()
    for dy in (1, 2, 3):
        w_copy(dy).wait_recv()
    accumulate(0)
    gather(4)
    spread(2)
    spread_far(2)
    accumulate(1)
    spread(3)
    spread_far(3)
    finish(2)
    spread(4)
    spread_far(4)
    sent_kv(1)
    sent_kv(2)
    for dy in (1, 2, 3):
        w_copy(dy).wait_send()
    sent_piece(0)
    sent_piece(1)
    finish(3)
    finish(4)
    for p in (2, 3, 4):
        sent_piece(p)


def shards(
    hidden_states, modulation, w_query, w_key, w_value, w_out, block_ids, block_count, guidance
):
    width = hidden_states.shape[2]
    bf16 = jnp.bfloat16
    dma = pltpu.SemaphoreType.DMA
    any_spec = pl.BlockSpec(memory_space=pltpu.HBM)
    vmem_spec = pl.BlockSpec(memory_space=pltpu.VMEM)
    per_round = pltpu.VMEM((ROUNDS, NZ, OWN_TILES, HD, TILE), bf16)
    pairs = []
    count = len(PIECES)
    for shape in (
        (ROUNDS, 3),
        (ROUNDS, 2, 2),
        (ROUNDS, 3),
        (count, 3),
        (3,),
        (3,),
        (count, 3),
        (count, 4),
        (2,),
        (count, 2),
    ):
        pairs += [dma(shape), dma(shape)]
    return pl.pallas_call(
        block_kernel,
        out_shape=jax.ShapeDtypeStruct((TOK, TOK), bf16),
        in_specs=[any_spec, vmem_spec]
        + [any_spec] * 4
        + [vmem_spec] * 3,
        out_specs=vmem_spec,
        scratch_shapes=[
            pltpu.VMEM((TOK, width), bf16),
            pltpu.VMEM((TOK, width), bf16),
            pltpu.VMEM((3 * ROUNDS, width, GROUP), bf16),
            pltpu.VMEM((ROUNDS, NZ, OWN_TILES, 2, HD, TILE), bf16),
            pltpu.VMEM((3 * SLAB, 2, HD, TILE), bf16),
            pltpu.VMEM((3 * SLAB, 2, HD, TILE), bf16),
            pltpu.VMEM((3 * SLAB, 2, HD, TILE), bf16),
            per_round,
            per_round,
            per_round,
            per_round,
            pltpu.VMEM((SLAB, SLOTS // 2, TILE, 2 * TILE), jnp.float32),
            pltpu.VMEM((NY, ROUNDS * GROUP, TOK), bf16),
            pltpu.VMEM((2, NY, ROUNDS, TOK, GROUP), bf16),
            pltpu.VMEM((2, TOK, TOK), jnp.float32),
            pltpu.VMEM((TOK, TOK), bf16),
            pltpu.VMEM((3, 1, width), jnp.float32),
            pltpu.VMEM((8, 128), jnp.int32),
            pltpu.VMEM((NZ, 8, 128), jnp.int32),
            pltpu.SMEM((NZ, 8, 128), jnp.int32),
            dma((13,)),
            *pairs,
            dma((4,)),
        ],
        compiler_params=pltpu.CompilerParams(
            collective_id=0, has_side_effects=True, vmem_limit_bytes=60 * 2**20
        ),
        name="block",
    )(
        hidden_states,
        jnp.transpose(modulation, (1, 0, 2)),
        w_query,
        w_key,
        w_value,
        w_out,
        block_ids,
        block_count.reshape(1, -1),
        guidance.reshape(1, 1),
    )


def solution(mesh):
    in_specs = (
        P("guid", "seq", None),
        P("guid", None, None),
        P(None, "tp"),
        P(None, "tp"),
        P(None, "tp"),
        P("tp", None),
        P("seq", None),
        P("seq"),
        P(),
    )
    out_specs = P("seq", ("guid", "tp"))
    return jax.shard_map(shards, mesh=mesh, in_specs=in_specs, out_specs=out_specs, check_vma=False)
```

```python
import functools

import jax
import jax.numpy as jnp
from jax import lax
from jax.experimental import pallas as pl
from jax.experimental.pallas import tpu as pltpu
from jax.sharding import PartitionSpec as P

HD = 64
TILE = 128
MESH = pl.DeviceIdType.MESH

NZ = 4
NY = 4
OWN_TILES = 3
SLAB = NZ * OWN_TILES
ROUNDS = 3
SLOTS = 12
TOK = OWN_TILES * TILE
GROUP = NZ * HD
PIECES = ((0, 0, 3), (1, 0, 3), (2, 0, 1), (2, 1, 1), (2, 2, 1))


def block_kernel(
    x_hbm,
    mod_ref,
    wq_hbm,
    wk_hbm,
    wv_hbm,
    wo_hbm,
    ids_ref,
    count_ref,
    guidance_ref,
    out_ref,
    xbuf,
    hbuf,
    wbuf,
    stage,
    kv_0,
    kv_1,
    kv_2,
    qstage,
    qbuf,
    ret,
    back,
    scores,
    wo,
    abuf,
    acc,
    xother,
    modother,
    meta,
    meta_all,
    meta_smem,
    load_sem,
    z_send,
    z_recv,
    x_send,
    x_recv,
    q_send,
    q_recv,
    r_send,
    r_recv,
    m_send,
    m_recv,
    w_send,
    w_recv,
    y_send,
    y_recv,
    c_send,
    c_recv,
    p_send,
    p_recv,
    f_send,
    f_recv,
    local_sem,
):
    seq = lax.axis_index("seq")
    guid = lax.axis_index("guid")
    tp = lax.axis_index("tp")
    px = seq // NZ
    pz = seq % NZ
    kv = (kv_0, kv_1, kv_2)

    def z_peer(dz):
        return (px * NZ + (pz + dz) % NZ, guid, tp)

    def x_peer(dx):
        return (((px + dx + NZ) % NZ) * NZ + pz, guid, tp)

    def y_peer(dy):
        return (seq, guid, (tp + dy) % NY)

    partner = (seq, 1 - guid, tp)

    def x_load(i):
        rows = pl.ds(i * TILE, TILE)
        return pltpu.make_async_copy(x_hbm.at[0, rows], xbuf.at[rows], load_sem.at[9 + i])

    def w_load(kind, j):
        source = (wq_hbm, wk_hbm, wv_hbm)[kind]
        slot = kind * ROUNDS + j
        return pltpu.make_async_copy(
            source.at[:, pl.ds(j * GROUP, GROUP)], wbuf.at[slot], load_sem.at[slot]
        )

    for i in range(OWN_TILES):
        x_load(i).start()
    w_load(1, 0).start()
    w_load(2, 0).start()

    wo_own = pltpu.make_async_copy(
        wo_hbm.at[:, pl.ds(pl.multiple_of((guid * NY + tp) * TOK, TILE), TOK)],
        wo.at[tp],
        load_sem.at[12],
    )

    meta[...] = jnp.zeros_like(meta)
    meta[0:3, 0:SLOTS] = ids_ref[...]
    meta[3:4, 0:3] = count_ref[...]
    meta_all[pz] = meta[...]

    barrier = pltpu.get_barrier_semaphore()
    peers = [z_peer(dz) for dz in (1, 2, 3)] + [x_peer(dx) for dx in (1, -1)]
    peers += [y_peer(dy) for dy in (1, 2, 3)] + [partner]
    for peer in peers:
        pl.semaphore_signal(barrier, inc=1, device_id=peer, device_id_type=MESH)
    pl.semaphore_wait(barrier, len(peers))

    def meta_copy(dz):
        return pltpu.make_async_remote_copy(
            src_ref=meta,
            dst_ref=meta_all.at[pz],
            send_sem=m_send.at[dz - 1],
            recv_sem=m_recv.at[dz - 1],
            device_id=z_peer(dz),
            device_id_type=MESH,
        )

    def z_copy(j, dz):
        return pltpu.make_async_remote_copy(
            src_ref=stage.at[j, (pz + dz) % NZ],
            dst_ref=kv[j].at[pl.ds(SLAB + (NZ - dz) * OWN_TILES, OWN_TILES)],
            send_sem=z_send.at[j, dz - 1],
            recv_sem=z_recv.at[j, dz - 1],
            device_id=z_peer(dz),
            device_id_type=MESH,
        )

    def own_copy(j):
        return pltpu.make_async_copy(
            stage.at[j, pz], kv[j].at[pl.ds(SLAB, OWN_TILES)], local_sem.at[j]
        )

    def x_copy_of(j, rest, side):
        first_slot, count = (OWN_TILES, SLAB - OWN_TILES) if rest else (0, OWN_TILES)
        return pltpu.make_async_remote_copy(
            src_ref=kv[j].at[pl.ds(SLAB + first_slot, count)] if rest else stage.at[j, pz],
            dst_ref=kv[j].at[pl.ds(2 * SLAB * side + first_slot, count)],
            send_sem=x_send.at[j, rest, side],
            recv_sem=x_recv.at[j, rest, side],
            device_id=x_peer(1 - 2 * side),
            device_id_type=MESH,
        )

    def q_copy(j, dz):
        return pltpu.make_async_remote_copy(
            src_ref=qstage.at[j, (pz + dz) % NZ],
            dst_ref=qbuf.at[j, pz],
            send_sem=q_send.at[j, dz - 1],
            recv_sem=q_recv.at[j, dz - 1],
            device_id=z_peer(dz),
            device_id_type=MESH,
        )

    def r_copy(p, dz):
        j, first_tile, count = PIECES[p]
        tiles = pl.ds(first_tile, count)
        return pltpu.make_async_remote_copy(
            src_ref=ret.at[j, (pz + dz) % NZ, tiles],
            dst_ref=back.at[j, pz, tiles],
            send_sem=r_send.at[p, dz - 1],
            recv_sem=r_recv.at[p, dz - 1],
            device_id=z_peer(dz),
            device_id_type=MESH,
        )

    def w_copy(dy):
        column = (guid * NY + (tp + dy) % NY) * TOK
        return pltpu.make_async_remote_copy(
            src_ref=wo_hbm.at[:, pl.ds(pl.multiple_of(column, TILE), TOK)],
            dst_ref=wo.at[tp],
            send_sem=w_send.at[dy - 1],
            recv_sem=w_recv.at[dy - 1],
            device_id=y_peer(dy),
            device_id_type=MESH,
        )

    def y_copy(p, dy):
        j, first_tile, count = PIECES[p]
        part = abuf.at[guid, tp, j, pl.ds(first_tile * TILE, count * TILE)]
        return pltpu.make_async_remote_copy(
            src_ref=part,
            dst_ref=part,
            send_sem=y_send.at[p, dy - 1],
            recv_sem=y_recv.at[p, dy - 1],
            device_id=y_peer(dy),
            device_id_type=MESH,
        )

    def f_copy(p, way):
        j, first_tile, count = PIECES[p]
        step = 1 - 2 * way
        size = count * TILE // 2
        half = abuf.at[
            guid, (tp - step + NY) % NY, j, pl.ds(first_tile * TILE + way * size, size)
        ]
        return pltpu.make_async_remote_copy(
            src_ref=half,
            dst_ref=half,
            send_sem=f_send.at[p, way],
            recv_sem=f_recv.at[p, way],
            device_id=y_peer((step + NY) % NY),
            device_id_type=MESH,
        )

    def c_copy(p, dy):
        j, first_tile, count = PIECES[p]
        origin = (tp - dy + NY) % NY
        part = abuf.at[guid, origin, j, pl.ds(first_tile * TILE, count * TILE)]
        return pltpu.make_async_remote_copy(
            src_ref=part,
            dst_ref=part,
            send_sem=c_send.at[p, dy],
            recv_sem=c_recv.at[p, dy],
            device_id=partner,
            device_id_type=MESH,
        )

    def p_copy(which):
        if which == 0:
            column = ((1 - guid) * NY + tp) * TOK
            source, target = xbuf.at[:, pl.ds(pl.multiple_of(column, TILE), TOK)], xother
        else:
            source, target = mod_ref, modother
        return pltpu.make_async_remote_copy(
            src_ref=source,
            dst_ref=target,
            send_sem=p_send.at[which],
            recv_sem=p_recv.at[which],
            device_id=partner,
            device_id_type=MESH,
        )

    rows = 16
    gain = 1.0 + mod_ref[1]
    for i in range(OWN_TILES):
        x_load(i).wait()
        if i == 0:
            w_load(1, 1).start()
            w_load(2, 1).start()
        if i == 1:
            w_load(1, 2).start()
            w_load(2, 2).start()

        def norm_rows(n, carry, i=i):
            at = pl.ds(pl.multiple_of(i * TILE + n * rows, rows), rows)
            xf = xbuf[at, :].astype(jnp.float32)
            width = xf.shape[1]
            mean = jnp.sum(xf, axis=1, keepdims=True) * (1.0 / width)
            off = xf - mean
            var = jnp.sum(off * off, axis=1, keepdims=True) * (1.0 / width)
            scale = 1.0 / jnp.sqrt(var + 1e-05)
            hbuf[at, :] = (off * scale * gain + mod_ref[0]).astype(jnp.bfloat16)
            return carry

        lax.fori_loop(0, TILE // rows, norm_rows, 0, unroll=8)
    for j in range(ROUNDS):
        w_load(0, j).start()

    def product(slot):
        w_load(slot // ROUNDS, slot % ROUNDS).wait()
        full = jnp.dot(hbuf[...], wbuf[slot], preferred_element_type=jnp.float32)
        return full.astype(jnp.bfloat16)

    def tiles_of(full):
        for i in range(OWN_TILES):
            part = full[i * TILE : (i + 1) * TILE, :]
            yield i, jnp.transpose(part).reshape(NZ, HD, TILE)

    def make_kv(j):
        for which in (0, 1):
            for i, part in tiles_of(product((1 + which) * ROUNDS + j)):
                stage[j, :, i, which] = part

    def z_arrived(j):
        for dz in (1, 3, 2):
            z_copy(j, dz).wait_recv()

    def forward(j):
        for side in (0, 1):
            x_copy_of(j, 1, side).start()

    def make_q(j):
        for i, part in tiles_of(product(j)):
            qstage[j, :, i] = part
        qbuf[j, pz] = qstage[j, pz]

    def send_z(j):
        for dz in (1, 3, 2):
            z_copy(j, dz).start()

    def send_q(j):
        for dz in (1, 3, 2):
            q_copy(j, dz).start()

    for j in range(ROUNDS):
        make_kv(j)
        if j == 0:
            send_z(0)
        for side in (0, 1):
            x_copy_of(j, 0, side).start()
        own_copy(j).start()
        if j == 0:
            for dz in (1, 2, 3):
                meta_copy(dz).start()
            for which in (0, 1):
                p_copy(which).start()
            for dy in (1, 3, 2):
                w_copy(dy).start()
    wo_own.start()
    make_q(0)
    z_arrived(0)
    send_z(1)
    send_q(0)
    forward(0)
    make_q(1)
    make_q(2)
    z_arrived(1)
    send_z(2)
    send_q(1)
    send_q(2)
    forward(1)
    z_arrived(2)
    forward(2)

    for dz in (1, 2, 3):
        meta_copy(dz).wait_recv()
    listed = meta_all[...]
    block = (listed * 171) >> 9
    slab = jnp.clip((block >> 2) - px + 1, 0, 2)
    slot = slab * SLAB + ((block - pz) & 3) * OWN_TILES + (listed - 3 * block)
    slot = jnp.clip(slot, 0, 3 * SLAB - 1)
    row = lax.broadcasted_iota(jnp.int32, listed.shape, 1)
    meta_all[...] = jnp.where(row == 3, listed, slot)
    meta_load = pltpu.make_async_copy(meta_all, meta_smem, local_sem.at[3])
    meta_load.start()
    meta_load.wait()

    one_rows = jnp.ones((HD, TILE), jnp.bfloat16)
    zero_rows = jnp.zeros((HD, TILE), jnp.bfloat16)

    def attend(j, owner, i, spot_of):
        q = jnp.transpose(qbuf[j, owner, i]) * jnp.asarray(0.125, jnp.bfloat16)
        top = None
        where = []
        for c in range(0, SLOTS, 2):
            spots = [meta_smem[owner, i, c + e] for e in (0, 1)]
            where.append(spots)
            pair = jnp.concatenate([kv[j][spot, 0] for spot in spots], axis=1)
            s = jnp.dot(q, pair, preferred_element_type=jnp.float32)
            scores[spot_of, c // 2] = s
            top = s if top is None else jnp.maximum(top, s)
        top = jnp.max(top, axis=1, keepdims=True)
        live = meta_smem[owner, 3, i]
        acc = None
        for c in range(0, SLOTS, 2):
            p = jnp.exp(scores[spot_of, c // 2] - top).astype(jnp.bfloat16)
            sides = []
            for e in (0, 1):
                ok = (c + e) < live
                spot = where[c // 2][e]
                sides.append(
                    jnp.concatenate(
                        [
                            jnp.where(ok, kv[j][spot, 1], zero_rows),
                            jnp.where(ok, one_rows, zero_rows),
                        ],
                        axis=0,
                    )
                )
            values = jnp.concatenate(sides, axis=1)
            part = lax.dot_general(
                p, values, (((1,), (1,)), ((), ())), preferred_element_type=jnp.float32
            )
            acc = part if acc is None else acc + part
        both = jnp.transpose(acc)
        ret[j, owner, i] = (both[:HD] / both[HD:]).astype(jnp.bfloat16)

    def ready(j):
        own_copy(j).wait()
        for rest in (0, 1):
            for side in (0, 1):
                x_copy_of(j, rest, side).wait_recv()
        for dz in (1, 3, 2):
            q_copy(j, dz).wait_recv()

    def attention_piece(p):
        j, first_tile, count = PIECES[p]
        for step in range(NZ):
            owner = (pz + step + 1) % NZ
            for i in range(first_tile, first_tile + count):
                attend(j, owner, i, step * OWN_TILES + i)
        for dz in (1, 3, 2):
            r_copy(p, dz).start()
        tiles = pl.ds(first_tile, count)
        back[j, pz, tiles] = ret[j, pz, tiles]

    def direct(p):
        return PIECES[p][0] == ROUNDS - 1

    def gather(p):
        j, first_tile, count = PIECES[p]
        for dz in (1, 3, 2):
            r_copy(p, dz).wait_recv()
        for i in range(first_tile, first_tile + count):
            part = back[j, :, i].reshape(GROUP, TILE)
            abuf[guid, tp, j, pl.ds(i * TILE, TILE), :] = jnp.transpose(part)
        for dy in (1, 3, 2) if direct(p) else (1, 3):
            y_copy(p, dy).start()
        c_copy(p, 0).start()

    def spread(p):
        for dy in (1, 3):
            y_copy(p, dy).wait_recv()
            if not direct(p):
                f_copy(p, dy // 2).start()
            c_copy(p, dy).start()

    def spread_far(p):
        if direct(p):
            y_copy(p, 2).wait_recv()
        else:
            for way in (0, 1):
                f_copy(p, way).wait_recv()
        c_copy(p, 2).start()

    def arrived(p):
        for dy in (0, 1, 3, 2):
            c_copy(p, dy).wait_recv()

    def part_of(branch, p, y):
        j, first_tile, count = PIECES[p]
        return jnp.dot(
            abuf[branch, y, j, pl.ds(first_tile * TILE, count * TILE), :],
            wo[y, pl.ds(j * GROUP, GROUP), :],
            preferred_element_type=jnp.float32,
        )

    def accumulate(p):
        arrived(p)
        for branch in (0, 1):

            def one(y, carry, branch=branch):
                acc[branch] += part_of(branch, p, y)
                return carry

            lax.fori_loop(0, NY, one, 0)

    column = pl.ds(pl.multiple_of((guid * NY + tp) * TOK, TILE), TOK)

    def finish(p):
        j, first_tile, count = PIECES[p]
        at = pl.ds(first_tile * TILE, count * TILE)
        strength = guidance_ref[...]

        def total(branch):
            summed = acc[branch, at, :]
            for y in range(NY):
                summed = summed + part_of(branch, p, y)
            return summed

        own = xbuf[at, column].astype(jnp.float32) + mod_ref[2, :, column] * total(guid)
        arrived(p)
        other = xother[at, :].astype(jnp.float32) + modother[2, :, column] * total(1 - guid)
        cond = jnp.where(guid == 0, own, other)
        uncond = jnp.where(guid == 0, other, own)
        out_ref[at, :] = (uncond + strength * (cond - uncond)).astype(jnp.bfloat16)

    def sent_kv(j):
        for dz in (1, 2, 3):
            z_copy(j, dz).wait_send()
            q_copy(j, dz).wait_send()
        for rest in (0, 1):
            for side in (0, 1):
                x_copy_of(j, rest, side).wait_send()

    def sent_piece(p):
        for dz in (1, 2, 3):
            r_copy(p, dz).wait_send()
        for dy in (1, 3, 2) if direct(p) else (1, 3):
            y_copy(p, dy).wait_send()
        if not direct(p):
            for way in (0, 1):
                f_copy(p, way).wait_send()
        for dy in (0, 1, 2, 3):
            c_copy(p, dy).wait_send()

    acc[...] = jnp.zeros_like(acc)
    ready(0)
    attention_piece(0)
    gather(0)
    ready(1)
    attention_piece(1)
    for which in (0, 1):
        p_copy(which).wait_recv()
        p_copy(which).wait_send()
    for dz in (1, 2, 3):
        meta_copy(dz).wait_send()
    sent_kv(0)
    ready(2)
    attention_piece(2)
    spread(0)
    gather(1)
    attention_piece(3)
    gather(2)
    attention_piece(4)
    spread_far(0)
    gather(3)
    spread(1)
    wo_own.wait()
    for dy in (1, 2, 3):
        w_copy(dy).wait_recv()
    accumulate(0)
    gather(4)
    spread_far(1)
    spread(2)
    accumulate(1)
    spread(3)
    spread_far(2)
    finish(2)
    spread(4)
    spread_far(3)
    sent_kv(1)
    sent_kv(2)
    for dy in (1, 2, 3):
        w_copy(dy).wait_send()
    sent_piece(0)
    sent_piece(1)
    finish(3)
    spread_far(4)
    finish(4)
    for p in (2, 3, 4):
        sent_piece(p)


def shards(
    hidden_states, modulation, w_query, w_key, w_value, w_out, block_ids, block_count, guidance
):
    width = hidden_states.shape[2]
    bf16 = jnp.bfloat16
    dma = pltpu.SemaphoreType.DMA
    any_spec = pl.BlockSpec(memory_space=pltpu.HBM)
    vmem_spec = pl.BlockSpec(memory_space=pltpu.VMEM)
    per_round = pltpu.VMEM((ROUNDS, NZ, OWN_TILES, HD, TILE), bf16)
    pairs = []
    count = len(PIECES)
    for shape in (
        (ROUNDS, 3),
        (ROUNDS, 2, 2),
        (ROUNDS, 3),
        (count, 3),
        (3,),
        (3,),
        (count, 3),
        (count, 4),
        (2,),
        (count, 2),
    ):
        pairs += [dma(shape), dma(shape)]
    return pl.pallas_call(
        block_kernel,
        out_shape=jax.ShapeDtypeStruct((TOK, TOK), bf16),
        in_specs=[any_spec, vmem_spec]
        + [any_spec] * 4
        + [vmem_spec] * 3,
        out_specs=vmem_spec,
        scratch_shapes=[
            pltpu.VMEM((TOK, width), bf16),
            pltpu.VMEM((TOK, width), bf16),
            pltpu.VMEM((3 * ROUNDS, width, GROUP), bf16),
            pltpu.VMEM((ROUNDS, NZ, OWN_TILES, 2, HD, TILE), bf16),
            pltpu.VMEM((3 * SLAB, 2, HD, TILE), bf16),
            pltpu.VMEM((3 * SLAB, 2, HD, TILE), bf16),
            pltpu.VMEM((3 * SLAB, 2, HD, TILE), bf16),
            per_round,
            per_round,
            per_round,
            per_round,
            pltpu.VMEM((SLAB, SLOTS // 2, TILE, 2 * TILE), jnp.float32),
            pltpu.VMEM((NY, ROUNDS * GROUP, TOK), bf16),
            pltpu.VMEM((2, NY, ROUNDS, TOK, GROUP), bf16),
            pltpu.VMEM((2, TOK, TOK), jnp.float32),
            pltpu.VMEM((TOK, TOK), bf16),
            pltpu.VMEM((3, 1, width), jnp.float32),
            pltpu.VMEM((8, 128), jnp.int32),
            pltpu.VMEM((NZ, 8, 128), jnp.int32),
            pltpu.SMEM((NZ, 8, 128), jnp.int32),
            dma((13,)),
            *pairs,
            dma((4,)),
        ],
        compiler_params=pltpu.CompilerParams(
            collective_id=0, has_side_effects=True, vmem_limit_bytes=60 * 2**20
        ),
        name="block",
    )(
        hidden_states,
        jnp.transpose(modulation, (1, 0, 2)),
        w_query,
        w_key,
        w_value,
        w_out,
        block_ids,
        block_count.reshape(1, -1),
        guidance.reshape(1, 1),
    )


def solution(mesh):
    in_specs = (
        P("guid", "seq", None),
        P("guid", None, None),
        P(None, "tp"),
        P(None, "tp"),
        P(None, "tp"),
        P("tp", None),
        P("seq", None),
        P("seq"),
        P(),
    )
    out_specs = P("seq", ("guid", "tp"))
    return jax.shard_map(shards, mesh=mesh, in_specs=in_specs, out_specs=out_specs, check_vma=False)
```

```python
import functools

import jax
import jax.numpy as jnp
from jax import lax
from jax.experimental import pallas as pl
from jax.experimental.pallas import tpu as pltpu
from jax.sharding import PartitionSpec as P

HD = 64
TILE = 128
MESH = pl.DeviceIdType.MESH

NZ = 4
NY = 4
OWN_TILES = 3
SLAB = NZ * OWN_TILES
ROUNDS = 3
SLOTS = 12
TOK = OWN_TILES * TILE
GROUP = NZ * HD
PIECES = ((0, 0, 3), (1, 0, 3), (2, 0, 1), (2, 1, 1), (2, 2, 1))


def block_kernel(
    x_hbm,
    mod_ref,
    wq_hbm,
    wk_hbm,
    wv_hbm,
    wo_hbm,
    ids_ref,
    count_ref,
    guidance_ref,
    out_ref,
    xbuf,
    hbuf,
    wbuf,
    stage,
    kv_0,
    kv_1,
    kv_2,
    qstage,
    qbuf,
    ret,
    back,
    scores,
    wo,
    abuf,
    acc,
    xother,
    modother,
    meta,
    meta_all,
    meta_smem,
    load_sem,
    z_send,
    z_recv,
    x_send,
    x_recv,
    q_send,
    q_recv,
    r_send,
    r_recv,
    m_send,
    m_recv,
    w_send,
    w_recv,
    y_send,
    y_recv,
    c_send,
    c_recv,
    p_send,
    p_recv,
    f_send,
    f_recv,
    local_sem,
):
    seq = lax.axis_index("seq")
    guid = lax.axis_index("guid")
    tp = lax.axis_index("tp")
    px = seq // NZ
    pz = seq % NZ
    kv = (kv_0, kv_1, kv_2)

    def z_peer(dz):
        return (px * NZ + (pz + dz) % NZ, guid, tp)

    def x_peer(dx):
        return (((px + dx + NZ) % NZ) * NZ + pz, guid, tp)

    def y_peer(dy):
        return (seq, guid, (tp + dy) % NY)

    partner = (seq, 1 - guid, tp)

    def x_load(i):
        rows = pl.ds(i * TILE, TILE)
        return pltpu.make_async_copy(x_hbm.at[0, rows], xbuf.at[rows], load_sem.at[9 + i])

    def w_load(kind, j):
        source = (wq_hbm, wk_hbm, wv_hbm)[kind]
        slot = kind * ROUNDS + j
        return pltpu.make_async_copy(
            source.at[:, pl.ds(j * GROUP, GROUP)], wbuf.at[slot], load_sem.at[slot]
        )

    for i in range(OWN_TILES):
        x_load(i).start()
    w_load(1, 0).start()
    w_load(2, 0).start()

    wo_own = pltpu.make_async_copy(
        wo_hbm.at[:, pl.ds(pl.multiple_of((guid * NY + tp) * TOK, TILE), TOK)],
        wo.at[tp],
        load_sem.at[12],
    )

    meta[...] = jnp.zeros_like(meta)
    meta[0:3, 0:SLOTS] = ids_ref[...]
    meta[3:4, 0:3] = count_ref[...]
    meta_all[pz] = meta[...]

    barrier = pltpu.get_barrier_semaphore()
    peers = [z_peer(dz) for dz in (1, 2, 3)] + [x_peer(dx) for dx in (1, -1)]
    peers += [y_peer(dy) for dy in (1, 2, 3)] + [partner]
    for peer in peers:
        pl.semaphore_signal(barrier, inc=1, device_id=peer, device_id_type=MESH)
    pl.semaphore_wait(barrier, len(peers))

    def meta_copy(dz):
        return pltpu.make_async_remote_copy(
            src_ref=meta,
            dst_ref=meta_all.at[pz],
            send_sem=m_send.at[dz - 1],
            recv_sem=m_recv.at[dz - 1],
            device_id=z_peer(dz),
            device_id_type=MESH,
        )

    def z_copy(j, dz):
        return pltpu.make_async_remote_copy(
            src_ref=stage.at[j, (pz + dz) % NZ],
            dst_ref=kv[j].at[pl.ds(SLAB + (NZ - dz) * OWN_TILES, OWN_TILES)],
            send_sem=z_send.at[j, dz - 1],
            recv_sem=z_recv.at[j, dz - 1],
            device_id=z_peer(dz),
            device_id_type=MESH,
        )

    def own_copy(j):
        return pltpu.make_async_copy(
            stage.at[j, pz], kv[j].at[pl.ds(SLAB, OWN_TILES)], local_sem.at[j]
        )

    def x_copy_of(j, rest, side):
        first_slot, count = (OWN_TILES, SLAB - OWN_TILES) if rest else (0, OWN_TILES)
        return pltpu.make_async_remote_copy(
            src_ref=kv[j].at[pl.ds(SLAB + first_slot, count)] if rest else stage.at[j, pz],
            dst_ref=kv[j].at[pl.ds(2 * SLAB * side + first_slot, count)],
            send_sem=x_send.at[j, rest, side],
            recv_sem=x_recv.at[j, rest, side],
            device_id=x_peer(1 - 2 * side),
            device_id_type=MESH,
        )

    def q_copy(j, dz):
        return pltpu.make_async_remote_copy(
            src_ref=qstage.at[j, (pz + dz) % NZ],
            dst_ref=qbuf.at[j, pz],
            send_sem=q_send.at[j, dz - 1],
            recv_sem=q_recv.at[j, dz - 1],
            device_id=z_peer(dz),
            device_id_type=MESH,
        )

    def r_copy(p, dz):
        j, first_tile, count = PIECES[p]
        tiles = pl.ds(first_tile, count)
        return pltpu.make_async_remote_copy(
            src_ref=ret.at[j, (pz + dz) % NZ, tiles],
            dst_ref=back.at[j, pz, tiles],
            send_sem=r_send.at[p, dz - 1],
            recv_sem=r_recv.at[p, dz - 1],
            device_id=z_peer(dz),
            device_id_type=MESH,
        )

    def w_copy(dy):
        column = (guid * NY + (tp + dy) % NY) * TOK
        return pltpu.make_async_remote_copy(
            src_ref=wo_hbm.at[:, pl.ds(pl.multiple_of(column, TILE), TOK)],
            dst_ref=wo.at[tp],
            send_sem=w_send.at[dy - 1],
            recv_sem=w_recv.at[dy - 1],
            device_id=y_peer(dy),
            device_id_type=MESH,
        )

    def y_copy(p, dy):
        j, first_tile, count = PIECES[p]
        part = abuf.at[guid, tp, j, pl.ds(first_tile * TILE, count * TILE)]
        return pltpu.make_async_remote_copy(
            src_ref=part,
            dst_ref=part,
            send_sem=y_send.at[p, dy - 1],
            recv_sem=y_recv.at[p, dy - 1],
            device_id=y_peer(dy),
            device_id_type=MESH,
        )

    def f_copy(p, way):
        j, first_tile, count = PIECES[p]
        step = 1 - 2 * way
        size = count * TILE // 2
        half = abuf.at[
            guid, (tp - step + NY) % NY, j, pl.ds(first_tile * TILE + way * size, size)
        ]
        return pltpu.make_async_remote_copy(
            src_ref=half,
            dst_ref=half,
            send_sem=f_send.at[p, way],
            recv_sem=f_recv.at[p, way],
            device_id=y_peer((step + NY) % NY),
            device_id_type=MESH,
        )

    def c_copy(p, dy):
        j, first_tile, count = PIECES[p]
        origin = (tp - dy + NY) % NY
        part = abuf.at[guid, origin, j, pl.ds(first_tile * TILE, count * TILE)]
        return pltpu.make_async_remote_copy(
            src_ref=part,
            dst_ref=part,
            send_sem=c_send.at[p, dy],
            recv_sem=c_recv.at[p, dy],
            device_id=partner,
            device_id_type=MESH,
        )

    def p_copy(which):
        if which == 0:
            column = ((1 - guid) * NY + tp) * TOK
            source, target = xbuf.at[:, pl.ds(pl.multiple_of(column, TILE), TOK)], xother
        else:
            source, target = mod_ref, modother
        return pltpu.make_async_remote_copy(
            src_ref=source,
            dst_ref=target,
            send_sem=p_send.at[which],
            recv_sem=p_recv.at[which],
            device_id=partner,
            device_id_type=MESH,
        )

    for dy in (1, 3, 2):
        w_copy(dy).start()

    rows = 16
    gain = 1.0 + mod_ref[1]
    for i in range(OWN_TILES):
        x_load(i).wait()
        if i == 0:
            w_load(1, 1).start()
            w_load(2, 1).start()
        if i == 1:
            w_load(1, 2).start()
            w_load(2, 2).start()

        def norm_rows(n, carry, i=i):
            at = pl.ds(pl.multiple_of(i * TILE + n * rows, rows), rows)
            xf = xbuf[at, :].astype(jnp.float32)
            width = xf.shape[1]
            mean = jnp.sum(xf, axis=1, keepdims=True) * (1.0 / width)
            off = xf - mean
            var = jnp.sum(off * off, axis=1, keepdims=True) * (1.0 / width)
            scale = 1.0 / jnp.sqrt(var + 1e-05)
            hbuf[at, :] = (off * scale * gain + mod_ref[0]).astype(jnp.bfloat16)
            return carry

        lax.fori_loop(0, TILE // rows, norm_rows, 0, unroll=8)
    for j in range(ROUNDS):
        w_load(0, j).start()

    def product(slot):
        w_load(slot // ROUNDS, slot % ROUNDS).wait()
        full = jnp.dot(hbuf[...], wbuf[slot], preferred_element_type=jnp.float32)
        return full.astype(jnp.bfloat16)

    def tiles_of(full):
        for i in range(OWN_TILES):
            part = full[i * TILE : (i + 1) * TILE, :]
            yield i, jnp.transpose(part).reshape(NZ, HD, TILE)

    def make_kv(j):
        for which in (0, 1):
            for i, part in tiles_of(product((1 + which) * ROUNDS + j)):
                stage[j, :, i, which] = part

    def z_arrived(j):
        for dz in (1, 3, 2):
            z_copy(j, dz).wait_recv()

    def forward(j):
        for side in (0, 1):
            x_copy_of(j, 1, side).start()

    def make_q(j):
        for i, part in tiles_of(product(j)):
            qstage[j, :, i] = part
        qbuf[j, pz] = qstage[j, pz]

    def send_z(j):
        for dz in (1, 3, 2):
            z_copy(j, dz).start()

    def send_q(j):
        for dz in (1, 3, 2):
            q_copy(j, dz).start()

    def send_own(j):
        for side in (0, 1):
            x_copy_of(j, 0, side).start()

    make_kv(0)
    send_z(0)
    send_own(0)
    own_copy(0).start()
    for dz in (1, 2, 3):
        meta_copy(dz).start()
    for which in (0, 1):
        p_copy(which).start()
    make_kv(1)
    send_own(1)
    own_copy(1).start()
    make_kv(2)
    own_copy(2).start()
    wo_own.start()
    make_q(0)
    z_arrived(0)
    send_z(1)
    send_q(0)
    forward(0)
    make_q(1)
    make_q(2)
    for dz in (1, 2, 3):
        meta_copy(dz).wait_recv()
    listed = meta_all[...]
    block = (listed * 171) >> 9
    slab = jnp.clip((block >> 2) - px + 1, 0, 2)
    slot = slab * SLAB + ((block - pz) & 3) * OWN_TILES + (listed - 3 * block)
    slot = jnp.clip(slot, 0, 3 * SLAB - 1)
    row = lax.broadcasted_iota(jnp.int32, listed.shape, 1)
    meta_all[...] = jnp.where(row == 3, listed, slot)
    meta_load = pltpu.make_async_copy(meta_all, meta_smem, local_sem.at[3])
    meta_load.start()
    meta_load.wait()

    one_rows = jnp.ones((HD, TILE), jnp.bfloat16)
    zero_rows = jnp.zeros((HD, TILE), jnp.bfloat16)

    def attend(j, owner, i, spot_of):
        q = jnp.transpose(qbuf[j, owner, i]) * jnp.asarray(0.125, jnp.bfloat16)
        top = None
        where = []
        for c in range(0, SLOTS, 2):
            spots = [meta_smem[owner, i, c + e] for e in (0, 1)]
            where.append(spots)
            pair = jnp.concatenate([kv[j][spot, 0] for spot in spots], axis=1)
            s = jnp.dot(q, pair, preferred_element_type=jnp.float32)
            scores[spot_of, c // 2] = s
            top = s if top is None else jnp.maximum(top, s)
        top = jnp.max(top, axis=1, keepdims=True)
        live = meta_smem[owner, 3, i]
        acc = None
        for c in range(0, SLOTS, 2):
            p = jnp.exp(scores[spot_of, c // 2] - top).astype(jnp.bfloat16)
            sides = []
            for e in (0, 1):
                ok = (c + e) < live
                spot = where[c // 2][e]
                sides.append(
                    jnp.concatenate(
                        [
                            jnp.where(ok, kv[j][spot, 1], zero_rows),
                            jnp.where(ok, one_rows, zero_rows),
                        ],
                        axis=0,
                    )
                )
            values = jnp.concatenate(sides, axis=1)
            part = lax.dot_general(
                p, values, (((1,), (1,)), ((), ())), preferred_element_type=jnp.float32
            )
            acc = part if acc is None else acc + part
        both = jnp.transpose(acc)
        ret[j, owner, i] = (both[:HD] / both[HD:]).astype(jnp.bfloat16)

    def ready(j):
        own_copy(j).wait()
        for rest in (0, 1):
            for side in (0, 1):
                x_copy_of(j, rest, side).wait_recv()
        for dz in (1, 3, 2):
            q_copy(j, dz).wait_recv()

    def attention_piece(p):
        j, first_tile, count = PIECES[p]
        for step in range(NZ):
            owner = (pz + step + 1) % NZ
            for i in range(first_tile, first_tile + count):
                attend(j, owner, i, step * OWN_TILES + i)
        for dz in (1, 3, 2):
            r_copy(p, dz).start()
        tiles = pl.ds(first_tile, count)
        back[j, pz, tiles] = ret[j, pz, tiles]

    def direct(p):
        return PIECES[p][0] == ROUNDS - 1

    def gather(p):
        j, first_tile, count = PIECES[p]
        for dz in (1, 3, 2):
            r_copy(p, dz).wait_recv()
        for i in range(first_tile, first_tile + count):
            part = back[j, :, i].reshape(GROUP, TILE)
            abuf[guid, tp, j, pl.ds(i * TILE, TILE), :] = jnp.transpose(part)
        for dy in (1, 3, 2) if direct(p) else (1, 3):
            y_copy(p, dy).start()
        c_copy(p, 0).start()

    def spread(p):
        for dy in (1, 3):
            y_copy(p, dy).wait_recv()
            if not direct(p):
                f_copy(p, dy // 2).start()
            c_copy(p, dy).start()

    def spread_far(p):
        if direct(p):
            y_copy(p, 2).wait_recv()
        else:
            for way in (0, 1):
                f_copy(p, way).wait_recv()
        c_copy(p, 2).start()

    def arrived(p):
        for dy in (0, 1, 3, 2):
            c_copy(p, dy).wait_recv()

    def part_of(branch, p, y):
        j, first_tile, count = PIECES[p]
        return jnp.dot(
            abuf[branch, y, j, pl.ds(first_tile * TILE, count * TILE), :],
            wo[y, pl.ds(j * GROUP, GROUP), :],
            preferred_element_type=jnp.float32,
        )

    def accumulate(p):
        arrived(p)
        for branch in (0, 1):

            def one(y, carry, branch=branch):
                acc[branch] += part_of(branch, p, y)
                return carry

            lax.fori_loop(0, NY, one, 0)

    column = pl.ds(pl.multiple_of((guid * NY + tp) * TOK, TILE), TOK)

    def finish(p):
        j, first_tile, count = PIECES[p]
        at = pl.ds(first_tile * TILE, count * TILE)
        strength = guidance_ref[...]

        def total(branch):
            summed = acc[branch, at, :]
            for y in range(NY):
                summed = summed + part_of(branch, p, y)
            return summed

        own = xbuf[at, column].astype(jnp.float32) + mod_ref[2, :, column] * total(guid)
        arrived(p)
        other = xother[at, :].astype(jnp.float32) + modother[2, :, column] * total(1 - guid)
        cond = jnp.where(guid == 0, own, other)
        uncond = jnp.where(guid == 0, other, own)
        out_ref[at, :] = (uncond + strength * (cond - uncond)).astype(jnp.bfloat16)

    def sent_kv(j):
        for dz in (1, 2, 3):
            z_copy(j, dz).wait_send()
            q_copy(j, dz).wait_send()
        for rest in (0, 1):
            for side in (0, 1):
                x_copy_of(j, rest, side).wait_send()

    def sent_piece(p):
        for dz in (1, 2, 3):
            r_copy(p, dz).wait_send()
        for dy in (1, 3, 2) if direct(p) else (1, 3):
            y_copy(p, dy).wait_send()
        if not direct(p):
            for way in (0, 1):
                f_copy(p, way).wait_send()
        for dy in (0, 1, 2, 3):
            c_copy(p, dy).wait_send()

    acc[...] = jnp.zeros_like(acc)
    z_arrived(1)
    send_z(2)
    send_q(1)
    ready(0)
    forward(1)
    attention_piece(0)
    z_arrived(2)
    send_q(2)
    ready(1)
    send_own(2)
    forward(2)
    gather(0)
    attention_piece(1)
    for which in (0, 1):
        p_copy(which).wait_recv()
        p_copy(which).wait_send()
    for dz in (1, 2, 3):
        meta_copy(dz).wait_send()
    sent_kv(0)
    spread(0)
    gather(1)
    ready(2)
    attention_piece(2)
    spread_far(0)
    attention_piece(3)
    gather(2)
    attention_piece(4)
    gather(3)
    spread(1)
    wo_own.wait()
    for dy in (1, 2, 3):
        w_copy(dy).wait_recv()
    accumulate(0)
    gather(4)
    spread_far(1)
    spread(2)
    accumulate(1)
    spread(3)
    spread_far(2)
    finish(2)
    spread(4)
    spread_far(3)
    sent_kv(1)
    sent_kv(2)
    for dy in (1, 2, 3):
        w_copy(dy).wait_send()
    sent_piece(0)
    sent_piece(1)
    finish(3)
    spread_far(4)
    finish(4)
    for p in (2, 3, 4):
        sent_piece(p)


def shards(
    hidden_states, modulation, w_query, w_key, w_value, w_out, block_ids, block_count, guidance
):
    width = hidden_states.shape[2]
    bf16 = jnp.bfloat16
    dma = pltpu.SemaphoreType.DMA
    any_spec = pl.BlockSpec(memory_space=pltpu.HBM)
    vmem_spec = pl.BlockSpec(memory_space=pltpu.VMEM)
    per_round = pltpu.VMEM((ROUNDS, NZ, OWN_TILES, HD, TILE), bf16)
    pairs = []
    count = len(PIECES)
    for shape in (
        (ROUNDS, 3),
        (ROUNDS, 2, 2),
        (ROUNDS, 3),
        (count, 3),
        (3,),
        (3,),
        (count, 3),
        (count, 4),
        (2,),
        (count, 2),
    ):
        pairs += [dma(shape), dma(shape)]
    return pl.pallas_call(
        block_kernel,
        out_shape=jax.ShapeDtypeStruct((TOK, TOK), bf16),
        in_specs=[any_spec, vmem_spec]
        + [any_spec] * 4
        + [vmem_spec] * 3,
        out_specs=vmem_spec,
        scratch_shapes=[
            pltpu.VMEM((TOK, width), bf16),
            pltpu.VMEM((TOK, width), bf16),
            pltpu.VMEM((3 * ROUNDS, width, GROUP), bf16),
            pltpu.VMEM((ROUNDS, NZ, OWN_TILES, 2, HD, TILE), bf16),
            pltpu.VMEM((3 * SLAB, 2, HD, TILE), bf16),
            pltpu.VMEM((3 * SLAB, 2, HD, TILE), bf16),
            pltpu.VMEM((3 * SLAB, 2, HD, TILE), bf16),
            per_round,
            per_round,
            per_round,
            per_round,
            pltpu.VMEM((SLAB, SLOTS // 2, TILE, 2 * TILE), jnp.float32),
            pltpu.VMEM((NY, ROUNDS * GROUP, TOK), bf16),
            pltpu.VMEM((2, NY, ROUNDS, TOK, GROUP), bf16),
            pltpu.VMEM((2, TOK, TOK), jnp.float32),
            pltpu.VMEM((TOK, TOK), bf16),
            pltpu.VMEM((3, 1, width), jnp.float32),
            pltpu.VMEM((8, 128), jnp.int32),
            pltpu.VMEM((NZ, 8, 128), jnp.int32),
            pltpu.SMEM((NZ, 8, 128), jnp.int32),
            dma((13,)),
            *pairs,
            dma((4,)),
        ],
        compiler_params=pltpu.CompilerParams(
            collective_id=0, has_side_effects=True, vmem_limit_bytes=60 * 2**20
        ),
        name="block",
    )(
        hidden_states,
        jnp.transpose(modulation, (1, 0, 2)),
        w_query,
        w_key,
        w_value,
        w_out,
        block_ids,
        block_count.reshape(1, -1),
        guidance.reshape(1, 1),
    )


def solution(mesh):
    in_specs = (
        P("guid", "seq", None),
        P("guid", None, None),
        P(None, "tp"),
        P(None, "tp"),
        P(None, "tp"),
        P("tp", None),
        P("seq", None),
        P("seq"),
        P(),
    )
    out_specs = P("seq", ("guid", "tp"))
    return jax.shard_map(shards, mesh=mesh, in_specs=in_specs, out_specs=out_specs, check_vma=False)
```

```python
import functools

import jax
import jax.numpy as jnp
from jax import lax
from jax.experimental import pallas as pl
from jax.experimental.pallas import tpu as pltpu
from jax.sharding import PartitionSpec as P

HD = 64
TILE = 128
MESH = pl.DeviceIdType.MESH

NZ = 4
NY = 4
OWN_TILES = 3
SLAB = NZ * OWN_TILES
ROUNDS = 3
SLOTS = 12
TOK = OWN_TILES * TILE
GROUP = NZ * HD
PIECES = ((0, 0, 3), (1, 0, 3), (2, 0, 1), (2, 1, 1), (2, 2, 1))


def block_kernel(
    x_hbm,
    mod_ref,
    wq_hbm,
    wk_hbm,
    wv_hbm,
    wo_hbm,
    ids_ref,
    count_ref,
    guidance_ref,
    out_ref,
    xbuf,
    hbuf,
    wbuf,
    stage,
    kv_0,
    kv_1,
    kv_2,
    qstage,
    qbuf,
    ret,
    back,
    scores,
    wo,
    abuf,
    acc,
    xother,
    modother,
    meta,
    meta_all,
    meta_smem,
    load_sem,
    z_send,
    z_recv,
    x_send,
    x_recv,
    q_send,
    q_recv,
    r_send,
    r_recv,
    m_send,
    m_recv,
    w_send,
    w_recv,
    y_send,
    y_recv,
    c_send,
    c_recv,
    p_send,
    p_recv,
    f_send,
    f_recv,
    local_sem,
):
    seq = lax.axis_index("seq")
    guid = lax.axis_index("guid")
    tp = lax.axis_index("tp")
    px = seq // NZ
    pz = seq % NZ
    kv = (kv_0, kv_1, kv_2)

    def z_peer(dz):
        return (px * NZ + (pz + dz) % NZ, guid, tp)

    def x_peer(dx):
        return (((px + dx + NZ) % NZ) * NZ + pz, guid, tp)

    def y_peer(dy):
        return (seq, guid, (tp + dy) % NY)

    partner = (seq, 1 - guid, tp)

    def x_load(i):
        rows = pl.ds(i * TILE, TILE)
        return pltpu.make_async_copy(x_hbm.at[0, rows], xbuf.at[rows], load_sem.at[9 + i])

    def w_load(kind, j):
        source = (wq_hbm, wk_hbm, wv_hbm)[kind]
        slot = kind * ROUNDS + j
        return pltpu.make_async_copy(
            source.at[:, pl.ds(j * GROUP, GROUP)], wbuf.at[slot], load_sem.at[slot]
        )

    for i in range(OWN_TILES):
        x_load(i).start()
    w_load(1, 0).start()
    w_load(2, 0).start()

    wo_own = pltpu.make_async_copy(
        wo_hbm.at[:, pl.ds(pl.multiple_of((guid * NY + tp) * TOK, TILE), TOK)],
        wo.at[tp],
        load_sem.at[12],
    )

    meta[...] = jnp.zeros_like(meta)
    meta[0:3, 0:SLOTS] = ids_ref[...]
    meta[3:4, 0:3] = count_ref[...]
    meta_all[pz] = meta[...]

    barrier = pltpu.get_barrier_semaphore()
    peers = [z_peer(dz) for dz in (1, 2, 3)] + [x_peer(dx) for dx in (1, -1)]
    peers += [y_peer(dy) for dy in (1, 2, 3)] + [partner]
    for peer in peers:
        pl.semaphore_signal(barrier, inc=1, device_id=peer, device_id_type=MESH)
    pl.semaphore_wait(barrier, len(peers))

    def meta_copy(dz):
        return pltpu.make_async_remote_copy(
            src_ref=meta,
            dst_ref=meta_all.at[pz],
            send_sem=m_send.at[dz - 1],
            recv_sem=m_recv.at[dz - 1],
            device_id=z_peer(dz),
            device_id_type=MESH,
        )

    def z_copy(j, dz):
        return pltpu.make_async_remote_copy(
            src_ref=stage.at[j, (pz + dz) % NZ],
            dst_ref=kv[j].at[pl.ds(SLAB + (NZ - dz) * OWN_TILES, OWN_TILES)],
            send_sem=z_send.at[j, dz - 1],
            recv_sem=z_recv.at[j, dz - 1],
            device_id=z_peer(dz),
            device_id_type=MESH,
        )

    def own_copy(j):
        return pltpu.make_async_copy(
            stage.at[j, pz], kv[j].at[pl.ds(SLAB, OWN_TILES)], local_sem.at[j]
        )

    def x_copy_of(j, rest, side):
        first_slot, count = (OWN_TILES, SLAB - OWN_TILES) if rest else (0, OWN_TILES)
        return pltpu.make_async_remote_copy(
            src_ref=kv[j].at[pl.ds(SLAB + first_slot, count)] if rest else stage.at[j, pz],
            dst_ref=kv[j].at[pl.ds(2 * SLAB * side + first_slot, count)],
            send_sem=x_send.at[j, rest, side],
            recv_sem=x_recv.at[j, rest, side],
            device_id=x_peer(1 - 2 * side),
            device_id_type=MESH,
        )

    def q_copy(j, dz):
        return pltpu.make_async_remote_copy(
            src_ref=qstage.at[j, (pz + dz) % NZ],
            dst_ref=qbuf.at[j, pz],
            send_sem=q_send.at[j, dz - 1],
            recv_sem=q_recv.at[j, dz - 1],
            device_id=z_peer(dz),
            device_id_type=MESH,
        )

    def r_copy(p, dz):
        j, first_tile, count = PIECES[p]
        tiles = pl.ds(first_tile, count)
        return pltpu.make_async_remote_copy(
            src_ref=ret.at[j, (pz + dz) % NZ, tiles],
            dst_ref=back.at[j, pz, tiles],
            send_sem=r_send.at[p, dz - 1],
            recv_sem=r_recv.at[p, dz - 1],
            device_id=z_peer(dz),
            device_id_type=MESH,
        )

    def w_copy(dy):
        column = (guid * NY + (tp + dy) % NY) * TOK
        return pltpu.make_async_remote_copy(
            src_ref=wo_hbm.at[:, pl.ds(pl.multiple_of(column, TILE), TOK)],
            dst_ref=wo.at[tp],
            send_sem=w_send.at[dy - 1],
            recv_sem=w_recv.at[dy - 1],
            device_id=y_peer(dy),
            device_id_type=MESH,
        )

    def y_copy(p, dy):
        j, first_tile, count = PIECES[p]
        part = abuf.at[guid, tp, j, pl.ds(first_tile * TILE, count * TILE)]
        return pltpu.make_async_remote_copy(
            src_ref=part,
            dst_ref=part,
            send_sem=y_send.at[p, dy - 1],
            recv_sem=y_recv.at[p, dy - 1],
            device_id=y_peer(dy),
            device_id_type=MESH,
        )

    def f_copy(p, way):
        j, first_tile, count = PIECES[p]
        step = 1 - 2 * way
        size = count * TILE // 2
        half = abuf.at[
            guid, (tp - step + NY) % NY, j, pl.ds(first_tile * TILE + way * size, size)
        ]
        return pltpu.make_async_remote_copy(
            src_ref=half,
            dst_ref=half,
            send_sem=f_send.at[p, way],
            recv_sem=f_recv.at[p, way],
            device_id=y_peer((step + NY) % NY),
            device_id_type=MESH,
        )

    def c_copy(p, dy):
        j, first_tile, count = PIECES[p]
        origin = (tp - dy + NY) % NY
        part = abuf.at[guid, origin, j, pl.ds(first_tile * TILE, count * TILE)]
        return pltpu.make_async_remote_copy(
            src_ref=part,
            dst_ref=part,
            send_sem=c_send.at[p, dy],
            recv_sem=c_recv.at[p, dy],
            device_id=partner,
            device_id_type=MESH,
        )

    def p_copy(which):
        if which == 0:
            column = ((1 - guid) * NY + tp) * TOK
            source, target = xbuf.at[:, pl.ds(pl.multiple_of(column, TILE), TOK)], xother
        else:
            source, target = mod_ref, modother
        return pltpu.make_async_remote_copy(
            src_ref=source,
            dst_ref=target,
            send_sem=p_send.at[which],
            recv_sem=p_recv.at[which],
            device_id=partner,
            device_id_type=MESH,
        )

    for dy in (1, 3, 2):
        w_copy(dy).start()

    rows = 16
    gain = 1.0 + mod_ref[1]
    for i in range(OWN_TILES):
        x_load(i).wait()
        if i == 0:
            w_load(1, 1).start()
            w_load(2, 1).start()
        if i == 1:
            w_load(1, 2).start()
            w_load(2, 2).start()

        def norm_rows(n, carry, i=i):
            at = pl.ds(pl.multiple_of(i * TILE + n * rows, rows), rows)
            xf = xbuf[at, :].astype(jnp.float32)
            width = xf.shape[1]
            mean = jnp.sum(xf, axis=1, keepdims=True) * (1.0 / width)
            off = xf - mean
            var = jnp.sum(off * off, axis=1, keepdims=True) * (1.0 / width)
            scale = 1.0 / jnp.sqrt(var + 1e-05)
            hbuf[at, :] = (off * scale * gain + mod_ref[0]).astype(jnp.bfloat16)
            return carry

        lax.fori_loop(0, TILE // rows, norm_rows, 0, unroll=8)
    for j in range(ROUNDS):
        w_load(0, j).start()

    def product(slot):
        w_load(slot // ROUNDS, slot % ROUNDS).wait()
        full = jnp.dot(hbuf[...], wbuf[slot], preferred_element_type=jnp.float32)
        return full.astype(jnp.bfloat16)

    def tiles_of(full):
        for i in range(OWN_TILES):
            part = full[i * TILE : (i + 1) * TILE, :]
            yield i, jnp.transpose(part).reshape(NZ, HD, TILE)

    def make_kv(j):
        for which in (0, 1):
            for i, part in tiles_of(product((1 + which) * ROUNDS + j)):
                stage[j, :, i, which] = part

    def z_arrived(j):
        for dz in (1, 3, 2):
            z_copy(j, dz).wait_recv()

    def forward(j):
        for side in (0, 1):
            x_copy_of(j, 1, side).start()

    def make_q(j):
        for i, part in tiles_of(product(j)):
            qstage[j, :, i] = part
        qbuf[j, pz] = qstage[j, pz]

    def send_z(j):
        for dz in (1, 3, 2):
            z_copy(j, dz).start()

    def send_q(j):
        for dz in (1, 3, 2):
            q_copy(j, dz).start()

    def send_own(j):
        for side in (0, 1):
            x_copy_of(j, 0, side).start()

    make_kv(0)
    send_z(0)
    send_own(0)
    own_copy(0).start()
    for dz in (1, 2, 3):
        meta_copy(dz).start()
    for which in (0, 1):
        p_copy(which).start()
    make_kv(1)
    send_own(1)
    own_copy(1).start()
    make_kv(2)
    own_copy(2).start()
    wo_own.start()
    make_q(0)
    z_arrived(0)
    send_z(1)
    send_q(0)
    forward(0)
    make_q(1)
    make_q(2)
    for dz in (1, 2, 3):
        meta_copy(dz).wait_recv()
    listed = meta_all[...]
    block = (listed * 171) >> 9
    slab = jnp.clip((block >> 2) - px + 1, 0, 2)
    slot = slab * SLAB + ((block - pz) & 3) * OWN_TILES + (listed - 3 * block)
    slot = jnp.clip(slot, 0, 3 * SLAB - 1)
    row = lax.broadcasted_iota(jnp.int32, listed.shape, 1)
    meta_all[...] = jnp.where(row == 3, listed, slot)
    meta_load = pltpu.make_async_copy(meta_all, meta_smem, local_sem.at[3])
    meta_load.start()
    meta_load.wait()

    one_rows = jnp.ones((HD, TILE), jnp.bfloat16)
    zero_rows = jnp.zeros((HD, TILE), jnp.bfloat16)

    def attend(j, owner, i, spot_of):
        q = jnp.transpose(qbuf[j, owner, i]) * jnp.asarray(0.125, jnp.bfloat16)
        top = None
        where = []
        for c in range(0, SLOTS, 2):
            spots = [meta_smem[owner, i, c + e] for e in (0, 1)]
            where.append(spots)
            pair = jnp.concatenate([kv[j][spot, 0] for spot in spots], axis=1)
            s = jnp.dot(q, pair, preferred_element_type=jnp.float32)
            scores[spot_of, c // 2] = s
            top = s if top is None else jnp.maximum(top, s)
        top = jnp.max(top, axis=1, keepdims=True)
        live = meta_smem[owner, 3, i]
        acc = None
        for c in range(0, SLOTS, 2):
            p = jnp.exp(scores[spot_of, c // 2] - top).astype(jnp.bfloat16)
            sides = []
            for e in (0, 1):
                ok = (c + e) < live
                spot = where[c // 2][e]
                sides.append(
                    jnp.concatenate(
                        [
                            jnp.where(ok, kv[j][spot, 1], zero_rows),
                            jnp.where(ok, one_rows, zero_rows),
                        ],
                        axis=0,
                    )
                )
            values = jnp.concatenate(sides, axis=1)
            part = lax.dot_general(
                p, values, (((1,), (1,)), ((), ())), preferred_element_type=jnp.float32
            )
            acc = part if acc is None else acc + part
        both = jnp.transpose(acc)
        ret[j, owner, i] = (both[:HD] / both[HD:]).astype(jnp.bfloat16)

    def ready(j):
        own_copy(j).wait()
        for rest in (0, 1):
            for side in (0, 1):
                x_copy_of(j, rest, side).wait_recv()
        for dz in (1, 3, 2):
            q_copy(j, dz).wait_recv()

    def attention_piece(p):
        j, first_tile, count = PIECES[p]
        for step in range(NZ):
            owner = (pz + step + 1) % NZ
            for i in range(first_tile, first_tile + count):
                attend(j, owner, i, step * OWN_TILES + i)
        for dz in (1, 3, 2):
            r_copy(p, dz).start()
        tiles = pl.ds(first_tile, count)
        back[j, pz, tiles] = ret[j, pz, tiles]

    def direct(p):
        return PIECES[p][0] == ROUNDS - 1

    def gather(p):
        j, first_tile, count = PIECES[p]
        for dz in (1, 3, 2):
            r_copy(p, dz).wait_recv()
        for i in range(first_tile, first_tile + count):
            part = back[j, :, i].reshape(GROUP, TILE)
            abuf[guid, tp, j, pl.ds(i * TILE, TILE), :] = jnp.transpose(part)
        for dy in (1, 3, 2) if direct(p) else (1, 3):
            y_copy(p, dy).start()
        c_copy(p, 0).start()

    def spread(p):
        for dy in (1, 3):
            y_copy(p, dy).wait_recv()
            if not direct(p):
                f_copy(p, dy // 2).start()
            c_copy(p, dy).start()

    def spread_far(p):
        if direct(p):
            y_copy(p, 2).wait_recv()
        else:
            for way in (0, 1):
                f_copy(p, way).wait_recv()
        c_copy(p, 2).start()

    def arrived(p):
        for dy in (0, 1, 3, 2):
            c_copy(p, dy).wait_recv()

    def part_of(branch, p, y):
        j, first_tile, count = PIECES[p]
        return jnp.dot(
            abuf[branch, y, j, pl.ds(first_tile * TILE, count * TILE), :],
            wo[y, pl.ds(j * GROUP, GROUP), :],
            preferred_element_type=jnp.float32,
        )

    def accumulate(p):
        arrived(p)
        for branch in (0, 1):

            def one(y, carry, branch=branch):
                acc[branch] += part_of(branch, p, y)
                return carry

            lax.fori_loop(0, NY, one, 0)

    column = pl.ds(pl.multiple_of((guid * NY + tp) * TOK, TILE), TOK)

    def finish(p):
        j, first_tile, count = PIECES[p]
        at = pl.ds(first_tile * TILE, count * TILE)
        strength = guidance_ref[...]

        def total(branch):
            summed = acc[branch, at, :]
            for y in range(NY):
                summed = summed + part_of(branch, p, y)
            return summed

        own = xbuf[at, column].astype(jnp.float32) + mod_ref[2, :, column] * total(guid)
        arrived(p)
        other = xother[at, :].astype(jnp.float32) + modother[2, :, column] * total(1 - guid)
        cond = jnp.where(guid == 0, own, other)
        uncond = jnp.where(guid == 0, other, own)
        out_ref[at, :] = (uncond + strength * (cond - uncond)).astype(jnp.bfloat16)

    def sent_kv(j):
        for dz in (1, 2, 3):
            z_copy(j, dz).wait_send()
            q_copy(j, dz).wait_send()
        for rest in (0, 1):
            for side in (0, 1):
                x_copy_of(j, rest, side).wait_send()

    def sent_piece(p):
        for dz in (1, 2, 3):
            r_copy(p, dz).wait_send()
        for dy in (1, 3, 2) if direct(p) else (1, 3):
            y_copy(p, dy).wait_send()
        if not direct(p):
            for way in (0, 1):
                f_copy(p, way).wait_send()
        for dy in (0, 1, 2, 3):
            c_copy(p, dy).wait_send()

    acc[...] = jnp.zeros_like(acc)
    z_arrived(1)
    send_z(2)
    send_q(1)
    ready(0)
    forward(1)
    attention_piece(0)
    z_arrived(2)
    send_q(2)
    ready(1)
    send_own(2)
    forward(2)
    gather(0)
    attention_piece(1)
    for which in (0, 1):
        p_copy(which).wait_recv()
        p_copy(which).wait_send()
    for dz in (1, 2, 3):
        meta_copy(dz).wait_send()
    sent_kv(0)
    ready(2)
    attention_piece(2)
    gather(1)
    spread(0)
    attention_piece(3)
    gather(2)
    attention_piece(4)
    spread_far(0)
    gather(3)
    gather(4)
    spread(1)
    wo_own.wait()
    for dy in (1, 2, 3):
        w_copy(dy).wait_recv()
    accumulate(0)
    spread_far(1)
    spread(2)
    accumulate(1)
    spread(3)
    spread_far(2)
    finish(2)
    spread(4)
    spread_far(3)
    sent_kv(1)
    sent_kv(2)
    for dy in (1, 2, 3):
        w_copy(dy).wait_send()
    sent_piece(0)
    sent_piece(1)
    finish(3)
    spread_far(4)
    finish(4)
    for p in (2, 3, 4):
        sent_piece(p)


def shards(
    hidden_states, modulation, w_query, w_key, w_value, w_out, block_ids, block_count, guidance
):
    width = hidden_states.shape[2]
    bf16 = jnp.bfloat16
    dma = pltpu.SemaphoreType.DMA
    any_spec = pl.BlockSpec(memory_space=pltpu.HBM)
    vmem_spec = pl.BlockSpec(memory_space=pltpu.VMEM)
    per_round = pltpu.VMEM((ROUNDS, NZ, OWN_TILES, HD, TILE), bf16)
    pairs = []
    count = len(PIECES)
    for shape in (
        (ROUNDS, 3),
        (ROUNDS, 2, 2),
        (ROUNDS, 3),
        (count, 3),
        (3,),
        (3,),
        (count, 3),
        (count, 4),
        (2,),
        (count, 2),
    ):
        pairs += [dma(shape), dma(shape)]
    return pl.pallas_call(
        block_kernel,
        out_shape=jax.ShapeDtypeStruct((TOK, TOK), bf16),
        in_specs=[any_spec, vmem_spec]
        + [any_spec] * 4
        + [vmem_spec] * 3,
        out_specs=vmem_spec,
        scratch_shapes=[
            pltpu.VMEM((TOK, width), bf16),
            pltpu.VMEM((TOK, width), bf16),
            pltpu.VMEM((3 * ROUNDS, width, GROUP), bf16),
            pltpu.VMEM((ROUNDS, NZ, OWN_TILES, 2, HD, TILE), bf16),
            pltpu.VMEM((3 * SLAB, 2, HD, TILE), bf16),
            pltpu.VMEM((3 * SLAB, 2, HD, TILE), bf16),
            pltpu.VMEM((3 * SLAB, 2, HD, TILE), bf16),
            per_round,
            per_round,
            per_round,
            per_round,
            pltpu.VMEM((SLAB, SLOTS // 2, TILE, 2 * TILE), jnp.float32),
            pltpu.VMEM((NY, ROUNDS * GROUP, TOK), bf16),
            pltpu.VMEM((2, NY, ROUNDS, TOK, GROUP), bf16),
            pltpu.VMEM((2, TOK, TOK), jnp.float32),
            pltpu.VMEM((TOK, TOK), bf16),
            pltpu.VMEM((3, 1, width), jnp.float32),
            pltpu.VMEM((8, 128), jnp.int32),
            pltpu.VMEM((NZ, 8, 128), jnp.int32),
            pltpu.SMEM((NZ, 8, 128), jnp.int32),
            dma((13,)),
            *pairs,
            dma((4,)),
        ],
        compiler_params=pltpu.CompilerParams(
            collective_id=0, has_side_effects=True, vmem_limit_bytes=60 * 2**20
        ),
        name="block",
    )(
        hidden_states,
        jnp.transpose(modulation, (1, 0, 2)),
        w_query,
        w_key,
        w_value,
        w_out,
        block_ids,
        block_count.reshape(1, -1),
        guidance.reshape(1, 1),
    )


def solution(mesh):
    in_specs = (
        P("guid", "seq", None),
        P("guid", None, None),
        P(None, "tp"),
        P(None, "tp"),
        P(None, "tp"),
        P("tp", None),
        P("seq", None),
        P("seq"),
        P(),
    )
    out_specs = P("seq", ("guid", "tp"))
    return jax.shard_map(shards, mesh=mesh, in_specs=in_specs, out_specs=out_specs, check_vma=False)
```
